32 devices in a mesh: fsdp: 4 (over x, core), ctx: 8 (over z, y).
Axes of the slice: x: 2, y: 2, z: 4, core: 2. Of those that a mesh axis runs over, the one named last changes fastest.
Arguments:
- tokens: bfloat16 [4, 2048, 1024], P('fsdp', 'ctx'), may hold values from -6 to 6
- out_grad: bfloat16 [4, 2048, 1024], P('fsdp', 'ctx'), may hold values from -6 to 6
- slot_block: int32 [4, 16], P('fsdp'), may hold values from 0 to 15, as said below
- w_attend: bfloat16 [1024, 3072], P('fsdp'), may hold values from -0.1875 to 0.1875
- w_mixing: bfloat16 [1024, 1024], P('fsdp'), may hold values from -1 to 1
- w_expand: bfloat16 [1024, 4096], P('fsdp'), may hold values from -0.1875 to 0.1875
- w_shrink: bfloat16 [4096, 1024], P('fsdp'), may hold values from -0.09375 to 0.09375
- w_norms: bfloat16 [4, 1024], P(None, 'fsdp'), may hold values from -1.2 to 1.4
- first_attend: float32 [1024, 3072], P('fsdp'), may hold values from -24 to 24
- first_mixing: float32 [1024, 1024], P('fsdp'), may hold values from -24 to 24
- first_expand: float32 [1024, 4096], P('fsdp'), may hold values from -24 to 24
- first_shrink: float32 [4096, 1024], P('fsdp'), may hold values from -24 to 24
- first_norms: float32 [4, 1024], P(None, 'fsdp'), may hold values from -24 to 24
- second_attend: float32 [1024, 3072], P('fsdp'), may hold values from 0.5 to 8
- second_mixing: float32 [1024, 1024], P('fsdp'), may hold values from 0.5 to 8
- second_expand: float32 [1024, 4096], P('fsdp'), may hold values from 0.5 to 8
- second_shrink: float32 [4096, 1024], P('fsdp'), may hold values from 0.5 to 8
- second_norms: float32 [4, 1024], P(None, 'fsdp'), may hold values from 0.5 to 8
Outputs:
- layer_out: bfloat16 [4, 2048, 1024], P('fsdp', 'ctx')
- tokens_grad: float32 [4, 2048, 1024], P('fsdp', 'ctx')
- grad_attend: float32 [1024, 3072], P('fsdp')
- update_attend: float32 [1024, 3072], P('fsdp')
- first_new_attend: float32 [1024, 3072], P('fsdp')
- second_new_attend: float32 [1024, 3072], P('fsdp')
- grad_mixing: float32 [1024, 1024], P('fsdp')
- update_mixing: float32 [1024, 1024], P('fsdp')
- first_new_mixing: float32 [1024, 1024], P('fsdp')
- second_new_mixing: float32 [1024, 1024], P('fsdp')
- grad_expand: float32 [1024, 4096], P('fsdp')
- update_expand: float32 [1024, 4096], P('fsdp')
- first_new_expand: float32 [1024, 4096], P('fsdp')
- second_new_expand: float32 [1024, 4096], P('fsdp')
- grad_shrink: float32 [4096, 1024], P('fsdp')
- update_shrink: float32 [4096, 1024], P('fsdp')
- first_new_shrink: float32 [4096, 1024], P('fsdp')
- second_new_shrink: float32 [4096, 1024], P('fsdp')
- grad_norms: float32 [4, 1024], P(None, 'fsdp')
- update_norms: float32 [4, 1024], P(None, 'fsdp')
- first_new_norms: float32 [4, 1024], P(None, 'fsdp')
- second_new_norms: float32 [4, 1024], P(None, 'fsdp')
The draws below stay inside these ranges and needn't reach their ends.
Inputs may be any that keep to these rules, and one draw needn't show every extreme that they name: `slot_block`: in each row every block number appears once, and slots 2i and 2i+1 hold two blocks whose numbers add up to 15.
All inputs are finite; a program needn't handle non-finite values.
Results may differ from the reference program's by a relative error of at most 0.025.
Values may be sent and summed in bfloat16 or wider, within the bound.
A program may use at most 256 MiB of HBM per device.

```python
import math
import jax
import jax.numpy as jnp
from jax import lax

D = 1024
H = 16
HD = 64
FF = 4096
LENGTH = 2048
STEP_COUNT = 10
SEQS = 4
N_CTX = 8


def draw_slot_block(key, part):

    def one_row(row_key):
        first, second = jax.random.split(row_key)
        order = jax.random.permutation(first, N_CTX).astype(jnp.int32)
        flip = jax.random.randint(second, (N_CTX,), 0, 2).astype(jnp.int32)
        late = 2 * N_CTX - 1 - order
        left = jnp.where(flip == 1, late, order)
        right = jnp.where(flip == 1, order, late)
        return jnp.stack([left, right], axis=1).reshape(2 * N_CTX).astype(jnp.int32)
    return jax.vmap(one_row)(jax.random.split(jax.random.fold_in(key, 11), SEQS))


def draw_w_norms(key, part):
    first, second = jax.random.split(jax.random.fold_in(key, 23))
    gains = jax.random.uniform(first, (2, D), jnp.float32, 0.6, 1.4)
    shifts = jnp.clip(0.3 * jax.random.normal(second, (2, D), jnp.float32), -1.2, 1.2)
    return jnp.stack([gains[0], shifts[0], gains[1], shifts[1]]).astype(jnp.bfloat16)


def levels(rng, dims, cuts, least, top_value):
    def one(position, shards_of):
        steps = jax.random.uniform(jax.random.fold_in(jax.random.fold_in(rng, 6), position), (shards_of,), jnp.float32, least / len(cuts), top_value / len(cuts))
        return jnp.repeat(jnp.exp(steps), dims[position] // shards_of).reshape((-1,) + (1,) * (len(dims) - position - 1))

    loudness = one(*cuts[0])
    for cut in cuts[1:]:
        loudness = loudness * one(*cut)
    return loudness


def noise(key, extent, width, most, cuts=(), kind=jnp.bfloat16):
    values = width * jax.random.normal(key, extent, jnp.float32)
    if cuts:
        values = values * levels(key, extent, cuts, -0.22, 0.18)
    return jnp.clip(values, -most, most).astype(kind)


def setup_inputs(seed: int = 0) -> dict:
    arg_keys = jax.random.split(jax.random.key(seed), 19)
    return {
        "tokens": noise(arg_keys[0], (SEQS, LENGTH, D), 1.0, 6.0, ((0, 4), (1, 8))),
        "out_grad": noise(arg_keys[1], (SEQS, LENGTH, D), 1.0, 6.0, ((0, 4), (1, 8))),
        "slot_block": draw_slot_block(jax.random.fold_in(arg_keys[18], 71), 0),
        "w_attend": noise(arg_keys[3], (D, 3 * D), D ** -0.5, 0.1875, ((0, 4),)),
        "w_mixing": noise(arg_keys[4], (D, D), (D * 64 // LENGTH) ** -0.5, 1.0, ((0, 4),)),
        "w_expand": noise(arg_keys[5], (D, FF), D ** -0.5, 0.1875, ((0, 4),)),
        "w_shrink": noise(arg_keys[6], (FF, D), FF ** -0.5, 0.09375, ((0, 4),)),
        "w_norms": draw_w_norms(jax.random.fold_in(arg_keys[18], 71), 0),
        "first_attend": noise(arg_keys[8], (D, 3 * D), 4.0, 24.0, ((0, 4),), jnp.float32),
        "first_mixing": noise(arg_keys[9], (D, D), 4.0, 24.0, ((0, 4),), jnp.float32),
        "first_expand": noise(arg_keys[10], (D, FF), 4.0, 24.0, ((0, 4),), jnp.float32),
        "first_shrink": noise(arg_keys[11], (FF, D), 4.0, 24.0, ((0, 4),), jnp.float32),
        "first_norms": noise(arg_keys[12], (4, D), 4.0, 24.0, ((1, 4),), jnp.float32),
        "second_attend": jnp.clip(jnp.exp(math.log(8.0) - 2.7725887 * jax.random.uniform(arg_keys[13], (D, 3 * D), jnp.float32) ** levels(arg_keys[13], (D, 3 * D), ((0, 4),), -0.2, 0.2)), 0.5, 8.0),
        "second_mixing": jnp.clip(jnp.exp(math.log(8.0) - 2.7725887 * jax.random.uniform(arg_keys[14], (D, D), jnp.float32) ** levels(arg_keys[14], (D, D), ((0, 4),), -0.2, 0.2)), 0.5, 8.0),
        "second_expand": jnp.clip(jnp.exp(math.log(8.0) - 2.7725887 * jax.random.uniform(arg_keys[15], (D, FF), jnp.float32) ** levels(arg_keys[15], (D, FF), ((0, 4),), -0.2, 0.2)), 0.5, 8.0),
        "second_shrink": jnp.clip(jnp.exp(math.log(8.0) - 2.7725887 * jax.random.uniform(arg_keys[16], (FF, D), jnp.float32) ** levels(arg_keys[16], (FF, D), ((0, 4),), -0.2, 0.2)), 0.5, 8.0),
        "second_norms": jnp.clip(jnp.exp(math.log(8.0) - 2.7725887 * jax.random.uniform(arg_keys[17], (4, D), jnp.float32) ** levels(arg_keys[17], (4, D), ((1, 4),), -0.2, 0.2)), 0.5, 8.0),
    }


EPS_NORM = 1e-05
NEG = -1e+30
BETA_ONE = 0.9
BETA_TWO = 0.999
LEARN = 0.02
DECAY = 0.1
EPS_ADAM = 1e-08
CUBIC = 0.044715
ROOT_TWO_PI = math.sqrt(2.0 / math.pi)
HIGH = lax.Precision.HIGHEST

@jax.custom_vjp
def low(v):
    return lax.optimization_barrier(v.astype(jnp.bfloat16)).astype(jnp.float32)

@jax.custom_vjp
def low_back(v):
    return v

def low_keep(v):
    return (low(v), None)

def low_pass(kept, grad):
    return (grad,)

def back_keep(v):
    return (v, None)

def back_low(kept, grad):
    return (low(grad),)
low.defvjp(low_keep, low_pass)
low_back.defvjp(back_keep, back_low)

def layer_norm(values, gain, shift):
    center = values - lax.optimization_barrier(jnp.mean(values, axis=-1, keepdims=True))
    spread = lax.optimization_barrier(jnp.mean(center * center, axis=-1, keepdims=True))
    return center * lax.rsqrt(spread + EPS_NORM) * gain + shift

def gelu(values):
    cube = values * values * values
    return 0.5 * values * (1.0 + jnp.tanh(ROOT_TWO_PI * (values + CUBIC * cube)))

def positions(slots, block):
    offsets = jnp.arange(block, dtype=jnp.int32)
    placed = slots[:, :, None] * block + offsets[None, None, :]
    return placed.reshape(slots.shape[0], slots.shape[1] * block).astype(jnp.int32)

def attend(query, keys, values, query_place, key_place):
    height = min(512, LENGTH)
    count = LENGTH // height
    scale = 1.0 / math.sqrt(HD)

    def one_block(inputs):
        piece, piece_place = inputs
        raw = jnp.einsum('qhd,khd->hqk', piece, keys, precision=HIGH) * scale
        raw = low_back(raw)
        allowed = key_place[None, None, :] <= piece_place[None, :, None]
        masked = jnp.where(allowed, raw, NEG)
        top = lax.optimization_barrier(jnp.max(masked, axis=-1, keepdims=True))
        total = top + jnp.log(lax.optimization_barrier(jnp.sum(jnp.exp(masked - top), axis=-1, keepdims=True)))
        probs = low(jnp.exp(masked - total))
        return jnp.einsum('hqk,khd->qhd', probs, values, precision=HIGH)
    result = lax.map(jax.checkpoint(one_block), (query.reshape(count, height, H, HD), query_place.reshape(count, height)))
    return result.reshape(LENGTH, D)

def adam_step(weight, grad, first, second):
    first_new = BETA_ONE * first + (1.0 - BETA_ONE) * grad
    second_new = BETA_TWO * second + (1.0 - BETA_TWO) * grad * grad
    mean_hat = first_new / (1.0 - BETA_ONE ** STEP_COUNT)
    square_hat = second_new / (1.0 - BETA_TWO ** STEP_COUNT)
    update = -LEARN * (mean_hat / (jnp.sqrt(square_hat) + EPS_ADAM) + DECAY * weight.astype(jnp.float32))
    return (update, first_new, second_new)

def reference(tokens, out_grad, slot_block, w_attend, w_mixing, w_expand, w_shrink, w_norms, first_attend, first_mixing, first_expand, first_shrink, first_norms, second_attend, second_mixing, second_expand, second_shrink, second_norms):
    places = positions(slot_block, LENGTH // (2 * N_CTX))

    def forward(inputs, attend_w, mixing_w, expand_w, shrink_w, norms_w):

        def one_sequence(carry, pair):
            sequence, place = pair
            normed = low(layer_norm(sequence, norms_w[0], norms_w[1]))
            joint = low_back(low(jnp.dot(normed, attend_w, precision=HIGH)))
            query = joint[:, :D].reshape(LENGTH, H, HD)
            keys = joint[:, D:2 * D].reshape(LENGTH, H, HD)
            values = joint[:, 2 * D:].reshape(LENGTH, H, HD)
            mixed = low_back(low(attend(query, keys, values, place, place)))
            branch = low_back(jnp.dot(mixed, mixing_w, precision=HIGH))
            middle = sequence + branch
            normed_two = low(layer_norm(middle, norms_w[2], norms_w[3]))
            expanded = low_back(jnp.dot(normed_two, expand_w, precision=HIGH))
            activated = low_back(low(gelu(expanded)))
            return (carry, middle + jnp.dot(activated, shrink_w, precision=HIGH))
        _, stacked = lax.scan(jax.checkpoint(one_sequence), None, (inputs, places))
        return stacked
    result, pull = jax.vjp(forward, tokens.astype(jnp.float32), w_attend.astype(jnp.float32), w_mixing.astype(jnp.float32), w_expand.astype(jnp.float32), w_shrink.astype(jnp.float32), w_norms.astype(jnp.float32))
    tokens_grad, grad_attend, grad_mixing, grad_expand, grad_shrink, grad_norms = pull(out_grad.astype(jnp.float32))
    layer_out = result.astype(jnp.bfloat16)
    update_attend, first_new_attend, second_new_attend = adam_step(w_attend, grad_attend, first_attend, second_attend)
    update_mixing, first_new_mixing, second_new_mixing = adam_step(w_mixing, grad_mixing, first_mixing, second_mixing)
    update_expand, first_new_expand, second_new_expand = adam_step(w_expand, grad_expand, first_expand, second_expand)
    update_shrink, first_new_shrink, second_new_shrink = adam_step(w_shrink, grad_shrink, first_shrink, second_shrink)
    update_norms, first_new_norms, second_new_norms = adam_step(w_norms, grad_norms, first_norms, second_norms)
    return (layer_out, tokens_grad, grad_attend, update_attend, first_new_attend, second_new_attend, grad_mixing, update_mixing, first_new_mixing, second_new_mixing, grad_expand, update_expand, first_new_expand, second_new_expand, grad_shrink, update_shrink, first_new_shrink, second_new_shrink, grad_norms, update_norms, first_new_norms, second_new_norms)
```

```python
import functools
import math

import jax
import jax.numpy as jnp
from jax import lax
from jax.experimental import pallas as pl
from jax.experimental.pallas import tpu as pltpu
from jax.sharding import PartitionSpec as P

HD = 64
STEP_COUNT = 10
EPS_NORM = 1e-05
NEG = -1e30
BETA_ONE = 0.9
BETA_TWO = 0.999
LEARN = 0.02
DECAY = 0.1
EPS_ADAM = 1e-08
CUBIC = 0.044715
ROOT_TWO_PI = math.sqrt(2.0 / math.pi)
LOG2E = math.log2(math.e)
TILE = 256
MESH = pl.DeviceIdType.MESH
F32 = jnp.float32
BF16 = jnp.bfloat16


def dot(left, right):
    return jnp.dot(left, right, preferred_element_type=F32)


def norm_parts(values):
    center = values - jnp.mean(values, axis=-1, keepdims=True)
    spread = jnp.mean(center * center, axis=-1, keepdims=True)
    inverse = lax.rsqrt(spread + EPS_NORM)
    return center * inverse, inverse


def norm_back(err, gain, normal, inverse):
    scaled = err * gain
    first = jnp.mean(scaled, axis=-1, keepdims=True)
    second = jnp.mean(scaled * normal, axis=-1, keepdims=True)
    return inverse * (scaled - first - normal * second)


def gelu_and_slope(values):
    square = values * values
    inner = ROOT_TWO_PI * values * (1.0 + CUBIC * square)
    tanh = jnp.tanh(inner)
    half = 0.5 * (1.0 + tanh)
    slope = half + 0.5 * values * (1.0 - tanh * tanh) * ROOT_TWO_PI * (
        1.0 + 3.0 * CUBIC * square
    )
    return values * half, slope


def adam_step(weight, grad, first, second):
    first_new = BETA_ONE * first + (1.0 - BETA_ONE) * grad
    second_new = BETA_TWO * second + (1.0 - BETA_TWO) * grad * grad
    mean_hat = first_new / (1.0 - BETA_ONE**STEP_COUNT)
    square_hat = second_new / (1.0 - BETA_TWO**STEP_COUNT)
    update = -LEARN * (
        mean_hat / (jnp.sqrt(square_hat) + EPS_ADAM) + DECAY * weight.astype(F32)
    )
    return (update, first_new, second_new)


def comm_call(kernel, out_shape, scratch, ident, operands, any_space=True):
    space = pl.ANY if any_space else pltpu.VMEM
    outs = jax.tree.map(lambda _: pl.BlockSpec(memory_space=space), out_shape)
    return pl.pallas_call(
        kernel,
        out_shape=out_shape,
        in_specs=[pl.BlockSpec(memory_space=space)] * len(operands),
        out_specs=outs,
        scratch_shapes=scratch,
        compiler_params=pltpu.CompilerParams(collective_id=ident, has_side_effects=True),
    )(*operands)


def remote(src, dst, send, recv, device):
    return pltpu.make_async_remote_copy(
        src_ref=src,
        dst_ref=dst,
        send_sem=send,
        recv_sem=recv,
        device_id=device,
        device_id_type=MESH,
    )


def fsdp_partners():
    f, c = lax.axis_index("fsdp"), lax.axis_index("ctx")
    x, k = f // 2, f % 2
    return f, c, x, k, x * 2 + 1 - k, (1 - x) * 2 + k


def greet(devices):
    barrier = pltpu.get_barrier_semaphore()
    for device in devices:
        pl.semaphore_signal(barrier, inc=1, device_id=device, device_id_type=MESH)
    pl.semaphore_wait(barrier, len(devices))


GATHER_CHUNKS = 4


def fsdp_gather_kernel(x_ref, o_ref, local_sem, send_sem, recv_sem):
    f, c, x, k, mate, across = fsdp_partners()
    mate_across = (1 - x) * 2 + 1 - k
    greet([(mate, c), (across, c)])
    rows = x_ref.shape[0]
    step = rows // GATHER_CHUNKS
    copies = []
    for t in range(GATHER_CHUNKS):
        part = pl.ds(t * step, step)
        copy = remote(
            x_ref.at[part],
            o_ref.at[f, part],
            send_sem.at[1, t],
            recv_sem.at[1, t],
            (across, c),
        )
        copy.start()
        copies.append(copy)
    near = remote(x_ref, o_ref.at[f], send_sem.at[0, 0], recv_sem.at[0, 0], (mate, c))
    near.start()
    local = pltpu.make_async_copy(x_ref, o_ref.at[f], local_sem)
    local.start()
    forwards = []
    for t in range(GATHER_CHUNKS):
        part = pl.ds(t * step, step)
        copies[t].wait_recv()
        forward = remote(
            o_ref.at[across, part],
            o_ref.at[across, part],
            send_sem.at[2, t],
            recv_sem.at[2, t],
            (mate, c),
        )
        forward.start()
        forwards.append(forward)
    local.wait()
    near.wait()
    for t in range(GATHER_CHUNKS):
        copies[t].wait_send()
        forwards[t].wait()


def fsdp_gather(values, ident, sizes):
    if sizes != (4, 8):
        return lax.all_gather(values, "fsdp", axis=0, tiled=False)
    return comm_call(
        fsdp_gather_kernel,
        jax.ShapeDtypeStruct((4,) + values.shape, values.dtype),
        [
            pltpu.SemaphoreType.DMA,
            pltpu.SemaphoreType.DMA((3, GATHER_CHUNKS)),
            pltpu.SemaphoreType.DMA((3, GATHER_CHUNKS)),
        ],
        ident,
        (values,),
    )


SCATTER_CHUNKS = 4


def fsdp_scatter_kernel(x_ref, o_ref, near_buf, far_out, far_in, send_sem, recv_sem):
    f, c, x, k, mate, across = fsdp_partners()
    greet([(mate, c), (across, c)])
    rows = x_ref.shape[1]
    step = rows // SCATTER_CHUNKS
    away = 1 - x
    near_far = []
    for t in range(SCATTER_CHUNKS):
        part = pl.ds(t * step, step)
        copy = remote(
            x_ref.at[away * 2 + 1 - k, part],
            near_buf.at[0, part],
            send_sem.at[0, t],
            recv_sem.at[0, t],
            (mate, c),
        )
        copy.start()
        near_far.append(copy)
    near_own = remote(
        x_ref.at[mate], near_buf.at[1], send_sem.at[2, 0], recv_sem.at[2, 0], (mate, c)
    )
    near_own.start()
    far = []
    for t in range(SCATTER_CHUNKS):
        part = pl.ds(t * step, step)
        near_far[t].wait_recv()
        far_out[part] = (
            x_ref[away * 2 + k, part].astype(F32) + near_buf[0, part].astype(F32)
        ).astype(BF16)
        copy = remote(
            far_out.at[part],
            far_in.at[part],
            send_sem.at[1, t],
            recv_sem.at[1, t],
            (across, c),
        )
        copy.start()
        far.append(copy)
    near_own.wait_recv()
    for t in range(SCATTER_CHUNKS):
        part = pl.ds(t * step, step)
        far[t].wait_recv()
        o_ref[part] = (
            x_ref[f, part].astype(F32)
            + near_buf[1, part].astype(F32)
            + far_in[part].astype(F32)
        )
    near_own.wait_send()
    for t in range(SCATTER_CHUNKS):
        near_far[t].wait_send()
        far[t].wait_send()


def fsdp_scatter(values, ident, sizes):
    if sizes != (4, 8):
        return lax.psum_scatter(
            values.astype(BF16), "fsdp", scatter_dimension=0, tiled=False
        ).astype(F32)
    rows, width = values.shape[1:]
    return comm_call(
        fsdp_scatter_kernel,
        jax.ShapeDtypeStruct((rows, width), F32),
        [
            pltpu.VMEM((2, rows, width), BF16),
            pltpu.VMEM((rows, width), BF16),
            pltpu.VMEM((rows, width), BF16),
            pltpu.SemaphoreType.DMA((3, SCATTER_CHUNKS)),
            pltpu.SemaphoreType.DMA((3, SCATTER_CHUNKS)),
        ],
        ident,
        (values,),
        any_space=False,
    )


def ctx_exchange_kernel(n, x_ref, o_ref, local_sem, send_sem, recv_sem):
    f, c = lax.axis_index("fsdp"), lax.axis_index("ctx")
    greet([(f, (c + j) % n) for j in range(1, n)])
    copies = []
    for j in range(n - 1, 0, -1):
        there = (c + j) % n
        copy = remote(
            x_ref.at[there], o_ref.at[c], send_sem.at[j], recv_sem.at[j], (f, there)
        )
        copy.start()
        copies.append(copy)
    local = pltpu.make_async_copy(x_ref.at[c], o_ref.at[c], local_sem)
    local.start()
    local.wait()
    for copy in copies:
        copy.wait()


def ctx_exchange(values, ident, sizes):
    if sizes != (4, 8):
        return lax.all_to_all(values, "ctx", split_axis=0, concat_axis=0, tiled=True)
    n = sizes[1]
    return comm_call(
        functools.partial(ctx_exchange_kernel, n),
        jax.ShapeDtypeStruct(values.shape, values.dtype),
        [
            pltpu.SemaphoreType.DMA,
            pltpu.SemaphoreType.DMA((n,)),
            pltpu.SemaphoreType.DMA((n,)),
        ],
        ident,
        (values,),
    )


def ctx_gather_kernel(cut, x_ref, o_ref, local_sem, send_sem, recv_sem):
    f, c = lax.axis_index("fsdp"), lax.axis_index("ctx")
    z, y = c // 2, c % 2
    depth = lax.axis_size("ctx") // 2
    rows = x_ref.shape[0]
    parts = (pl.ds(0, cut), pl.ds(cut, rows - cut))
    mate = z * 2 + 1 - y
    barrier = pltpu.get_barrier_semaphore()

    def signal(device):
        pl.semaphore_signal(barrier, inc=1, device_id=device, device_id_type=MESH)

    signal((f, mate))
    pl.when(z > 0)(lambda: signal((f, c - 2)))
    pl.when(z < depth - 1)(lambda: signal((f, c + 2)))
    pl.semaphore_wait(barrier, 1 + (z + depth - 1) // depth + (2 * depth - 2 - z) // depth)

    def copy(zz, yy, part, way, own=False):
        block = zz * 2 + yy
        src = x_ref.at[parts[part]] if own else o_ref.at[block, parts[part]]
        there = (c - 2, c + 2, mate)[way]
        return remote(
            src,
            o_ref.at[block, parts[part]],
            send_sem.at[block, part, way],
            recv_sem.at[block, part],
            (f, there),
        )

    local = pltpu.make_async_copy(x_ref, o_ref.at[c], local_sem)
    local.start()
    for part in (0, 1):
        pl.when(z < depth - 1)(lambda: copy(z, y, part, 1, True).start())
        pl.when(z > 0)(lambda: copy(z, y, part, 0, True).start())
    for part in (1, 0):
        copy(z, y, part, 2, True).start()
    local.wait()

    def arrive(zz, yy, part, way):
        copy(zz, yy, part, way).wait_recv()
        if way == 1:
            pl.when(z < depth - 1)(lambda: copy(zz, yy, part, 1).start())
        else:
            pl.when(z > 0)(lambda: copy(zz, yy, part, 0).start())
        if part == 0:
            copy(zz, yy, part, 2).start()

    def from_mate_second():
        copy(z, 1 - y, 1, 2).wait_recv()
        pl.when(z < depth - 1)(lambda: copy(z, 1 - y, 1, 1).start())
        pl.when(z > 0)(lambda: copy(z, 1 - y, 1, 0).start())

    def along(step, yy, part):
        pl.when(z - step >= 0)(lambda: arrive(z - step, yy, part, 1))
        pl.when(z + step < depth)(lambda: arrive(z + step, yy, part, 0))

    for step in range(1, depth):
        along(step, y, 0)
        along(step, y, 1)
        if step == 1:
            from_mate_second()
        along(step, 1 - y, 1)
    copy(z, 1 - y, 0, 2).wait_recv()
    for step in range(1, depth):
        pl.when(z - step >= 0)(lambda: copy(z - step, 1 - y, 0, 2).wait_recv())
        pl.when(z + step < depth)(lambda: copy(z + step, 1 - y, 0, 2).wait_recv())
    for step in range(depth):
        for yy, part in ((y, 0), (y, 1), (1 - y, 1)):

            def sent_right():
                copy(z - step, yy, part, 1).wait_send()

            def sent_left():
                copy(z + step, yy, part, 0).wait_send()

            pl.when((z - step >= 0) & (z < depth - 1))(sent_right)
            pl.when((z + step < depth) & (z > 0))(sent_left)
    copy(z, y, 0, 2).wait_send()
    copy(z, y, 1, 2).wait_send()
    for step in range(1, depth):
        pl.when(z - step >= 0)(lambda: copy(z - step, y, 0, 2).wait_send())
        pl.when(z + step < depth)(lambda: copy(z + step, y, 0, 2).wait_send())


def ctx_gather(values, ident, sizes):
    if sizes != (4, 8):
        return lax.all_gather(values, "ctx", axis=0, tiled=False)
    n = sizes[1]
    rows = values.shape[0]
    cut = rows * 5 // 8
    return comm_call(
        functools.partial(ctx_gather_kernel, cut),
        jax.ShapeDtypeStruct((n,) + values.shape, values.dtype),
        [
            pltpu.SemaphoreType.DMA,
            pltpu.SemaphoreType.DMA((n, 2, 3)),
            pltpu.SemaphoreType.DMA((n, 2)),
        ],
        ident,
        (values,),
    )


def head_rows(h):
    return slice(h * HD, (h + 1) * HD)


def attend_forward_kernel(
    heads, slot_ref, place_ref, qkv_ref, mixed_ref, out_t_ref, total_ref,
    q_pos, k_pos, v_pos, q_t, v_t, scores, o_pos,
):
    length, lanes = q_pos.shape
    blocks = slot_ref.shape[0]
    size = length // blocks
    tiles = length // TILE
    factor = LOG2E / math.sqrt(HD)
    for p in range(blocks):
        rows = qkv_ref[pl.ds(slot_ref[p] * size, size), :]
        here = slice(p * size, (p + 1) * size)
        q_pos[here, :] = rows[:, :lanes]
        k_pos[here, :] = rows[:, lanes : 2 * lanes]
        v_pos[here, :] = rows[:, 2 * lanes :]
    for t in range(tiles):
        here = slice(t * TILE, (t + 1) * TILE)
        q_t[:, here] = q_pos[here, :].T
        v_t[:, here] = v_pos[here, :].T
    head_of_row = lax.broadcasted_iota(jnp.int32, (lanes, TILE), 0) // HD
    allowed = lax.broadcasted_iota(jnp.int32, (TILE, TILE), 0) <= lax.broadcasted_iota(
        jnp.int32, (TILE, TILE), 1
    )

    def fold_max(values):
        return jnp.max(values.reshape(TILE // 8, 8, TILE), axis=0)

    def fold_sum(values):
        return jnp.sum(values.reshape(TILE // 8, 8, TILE), axis=0)

    @pl.loop(0, tiles)
    def _(i):
        here = pl.ds(pl.multiple_of(i * TILE, TILE), TILE)
        q_tile = q_t[:, here]
        q_heads = [
            jnp.where(head_of_row == h, q_tile, jnp.zeros_like(q_tile)) for h in range(heads)
        ]

        def first(j, tops):
            there = pl.ds(pl.multiple_of(j * TILE, TILE), TILE)
            keys = k_pos[there, :]
            result = []
            for h in range(heads):
                raw = dot(keys, q_heads[h])
                scores[h, there, :] = raw
                result.append(jnp.maximum(tops[h], fold_max(raw)))
            return tuple(result)

        tops = lax.fori_loop(
            0, i, first, tuple(jnp.full((8, TILE), NEG, F32) for _ in range(heads))
        )
        keys = k_pos[here, :]
        row_tops = []
        for h in range(heads):
            raw = jnp.where(allowed, dot(keys, q_heads[h]), NEG)
            scores[h, here, :] = raw
            row_tops.append(
                jnp.max(jnp.maximum(tops[h], fold_max(raw)), axis=0, keepdims=True) * factor
            )

        def second(j, state):
            there = pl.ds(pl.multiple_of(j * TILE, TILE), TILE)
            result = []
            for h in range(heads):
                sums, acc = state[h]
                probs = jnp.exp2(scores[h, there, :] * factor - row_tops[h])
                acc = acc + dot(v_t[head_rows(h), there], probs.astype(BF16))
                result.append((sums + fold_sum(probs), acc))
            return tuple(result)

        state = lax.fori_loop(
            0,
            i + 1,
            second,
            tuple(
                (jnp.zeros((8, TILE), F32), jnp.zeros((HD, TILE), F32)) for _ in range(heads)
            ),
        )
        outs = []
        for h in range(heads):
            sums, acc = state[h]
            row_sum = jnp.sum(sums, axis=0, keepdims=True)
            out = acc * (1.0 / row_sum)
            out_t_ref[head_rows(h), here] = out
            total_ref[pl.ds(h, 1), here] = row_tops[h] + jnp.log2(row_sum)
            outs.append(out)
        out = jnp.concatenate(outs, axis=0) if heads > 1 else outs[0]
        o_pos[here, :] = out.T.astype(BF16)

    for s in range(blocks):
        mixed_ref[s * size : (s + 1) * size, :] = o_pos[
            pl.ds(place_ref[s] * size, size), :
        ]


def attend_forward(slot_of, place_of, qkv, heads):
    length = qkv.shape[0]
    lanes = heads * HD
    vmem = pl.BlockSpec(memory_space=pltpu.VMEM)
    smem = pl.BlockSpec(memory_space=pltpu.SMEM)
    return pl.pallas_call(
        functools.partial(attend_forward_kernel, heads),
        out_shape=(
            jax.ShapeDtypeStruct((length, lanes), BF16),
            jax.ShapeDtypeStruct((lanes, length), F32),
            jax.ShapeDtypeStruct((8, length), F32),
        ),
        in_specs=[smem, smem, vmem],
        out_specs=(vmem, vmem, vmem),
        scratch_shapes=[pltpu.VMEM((length, lanes), BF16)] * 3
        + [pltpu.VMEM((lanes, length), BF16)] * 2
        + [pltpu.VMEM((heads, length, TILE), F32), pltpu.VMEM((length, lanes), BF16)],
        cost_estimate=pl.CostEstimate(
            flops=4 * length * length * lanes,
            bytes_accessed=10 * length * lanes,
            transcendentals=heads * length * length // 2,
        ),
    )(slot_of, place_of, qkv)


def attend_backward_kernel(
    heads, slot_ref, place_ref, qkv_ref, grad_ref, out_t_ref, total_ref, result_ref,
    q_pos, k_pos, v_pos, g_pos, k_heads, v_heads, q_t, k_t, g_t, delta,
    dq_t, dk_acc, dv_acc, d_pos,
):
    length, lanes = q_pos.shape
    blocks = slot_ref.shape[0]
    size = length // blocks
    tiles = length // TILE
    scale = 1.0 / math.sqrt(HD)
    factor = LOG2E * scale
    for p in range(blocks):
        rows = qkv_ref[pl.ds(slot_ref[p] * size, size), :]
        here = slice(p * size, (p + 1) * size)
        q_pos[here, :] = rows[:, :lanes]
        k_pos[here, :] = rows[:, lanes : 2 * lanes]
        v_pos[here, :] = rows[:, 2 * lanes :]
        g_pos[here, :] = grad_ref[pl.ds(slot_ref[p] * size, size), :]
    head_of_lane = lax.broadcasted_iota(jnp.int32, (TILE, lanes), 1) // HD
    allowed = lax.broadcasted_iota(jnp.int32, (TILE, TILE), 0) <= lax.broadcasted_iota(
        jnp.int32, (TILE, TILE), 1
    )
    for t in range(tiles):
        here = slice(t * TILE, (t + 1) * TILE)
        q_t[:, here] = q_pos[here, :].T
        k_t[:, here] = k_pos[here, :].T
        g_tile = g_pos[here, :].T
        g_t[:, here] = g_tile
        product = g_tile.astype(F32) * out_t_ref[:, here]
        for h in range(heads):
            delta[h : h + 1, here] = jnp.sum(product[head_rows(h)], axis=0, keepdims=True)
            keys, values = k_pos[here, :], v_pos[here, :]
            k_heads[h, here, :] = jnp.where(head_of_lane == h, keys, jnp.zeros_like(keys))
            v_heads[h, here, :] = jnp.where(head_of_lane == h, values, jnp.zeros_like(values))
    dq_t[...] = jnp.zeros_like(dq_t)

    def pair(j, i, masked):
        there = pl.ds(pl.multiple_of(j * TILE, TILE), TILE)
        here = pl.ds(pl.multiple_of(i * TILE, TILE), TILE)
        for h in range(heads):
            raw = dot(k_heads[h, there, :], q_t[:, here])
            probs = jnp.exp2(raw * factor - total_ref[pl.ds(h, 1), here])
            if masked:
                probs = jnp.where(allowed, probs, 0.0)
            d_probs = dot(v_heads[h, there, :], g_t[:, here])
            d_scores = (probs * (d_probs - delta[pl.ds(h, 1), here])).astype(BF16)
            dv = dot(probs.astype(BF16), g_pos[here, :])
            dk = dot(d_scores, q_pos[here, :])
            if masked:
                dv_acc[h], dk_acc[h] = dv, dk
            else:
                dv_acc[h] += dv
                dk_acc[h] += dk
            dq_t[head_rows(h), here] += dot(k_t[head_rows(h), there], d_scores)

    @pl.loop(0, tiles)
    def _(j):
        pair(j, j, True)

        @pl.loop(j + 1, tiles)
        def _(i):
            pair(j, i, False)

        there = pl.ds(pl.multiple_of(j * TILE, TILE), TILE)
        for index, acc, weight in ((1, dk_acc, scale), (2, dv_acc, 1.0)):
            value = acc[0]
            for h in range(1, heads):
                value = jnp.where(head_of_lane == h, acc[h], value)
            d_pos[there, index * lanes : (index + 1) * lanes] = (value * weight).astype(BF16)

    for t in range(tiles):
        here = slice(t * TILE, (t + 1) * TILE)
        d_pos[here, :lanes] = (dq_t[:, here].T * scale).astype(BF16)
    for s in range(blocks):
        result_ref[s * size : (s + 1) * size, :] = d_pos[pl.ds(place_ref[s] * size, size), :]


def attend_backward(slot_of, place_of, qkv, grad, out_t, total, heads):
    length = qkv.shape[0]
    lanes = heads * HD
    vmem = pl.BlockSpec(memory_space=pltpu.VMEM)
    smem = pl.BlockSpec(memory_space=pltpu.SMEM)
    rows = pltpu.VMEM((length, lanes), BF16)
    columns = pltpu.VMEM((lanes, length), BF16)
    by_head = pltpu.VMEM((heads, length, lanes), BF16)
    return pl.pallas_call(
        functools.partial(attend_backward_kernel, heads),
        out_shape=jax.ShapeDtypeStruct((length, 3 * lanes), BF16),
        in_specs=[smem, smem, vmem, vmem, vmem, vmem],
        out_specs=vmem,
        scratch_shapes=[rows] * 4
        + [by_head] * 2
        + [columns] * 3
        + [
            pltpu.VMEM((8, length), F32),
            pltpu.VMEM((lanes, length), F32),
            pltpu.VMEM((heads, TILE, lanes), F32),
            pltpu.VMEM((heads, TILE, lanes), F32),
            pltpu.VMEM((length, 3 * lanes), BF16),
        ],
        cost_estimate=pl.CostEstimate(
            flops=10 * length * length * lanes,
            bytes_accessed=20 * length * lanes,
            transcendentals=heads * length * length // 2,
        ),
    )(slot_of, place_of, qkv, grad, out_t, total)


def shards(
    sizes,
    tokens,
    out_grad,
    slot_block,
    w_attend,
    w_mixing,
    w_expand,
    w_shrink,
    w_norms,
    first_attend,
    first_mixing,
    first_expand,
    first_shrink,
    first_norms,
    second_attend,
    second_mixing,
    second_expand,
    second_shrink,
    second_norms,
):
    fsdp, ctx = sizes
    f, c = lax.axis_index("fsdp"), lax.axis_index("ctx")
    rows, width = tokens.shape[1:]
    heads = width // HD // ctx
    lanes = heads * HD
    length = rows * ctx
    own = width // fsdp
    hidden = w_shrink.shape[0]

    place_of = slot_block[0]
    slot_of = jnp.sum(
        jnp.where(
            place_of[None, :] == jnp.arange(2 * ctx, dtype=jnp.int32)[:, None],
            jnp.arange(2 * ctx, dtype=jnp.int32)[None, :],
            0,
        ),
        axis=1,
    )

    start = tokens[0]
    incoming = out_grad[0]
    attend_grouped = (
        w_attend.reshape(own, 3, ctx, lanes).transpose(0, 2, 1, 3).reshape(own, ctx, 3 * lanes)
    )
    attend_here = lax.dynamic_index_in_dim(attend_grouped, c, 1, keepdims=False)
    norms = lax.all_gather(w_norms, "fsdp", axis=1, tiled=True).astype(F32)
    whole_tokens = ctx_gather(start, 0, sizes).reshape(length, width)
    whole_here = fsdp_gather(attend_here, 1, sizes).reshape(width, 3 * lanes)
    whole_attend = lax.all_gather(
        attend_grouped.reshape(own, 3 * width), "fsdp", axis=0, tiled=True
    )
    whole_mixing = lax.all_gather(w_mixing, "fsdp", axis=0, tiled=True)
    expand_columns = lax.all_to_all(
        w_expand.reshape(own, fsdp, hidden).transpose(1, 0, 2),
        "fsdp",
        split_axis=0,
        concat_axis=0,
        tiled=True,
    ).reshape(width, hidden)
    grads_in = lax.all_gather(incoming, "fsdp", axis=0, tiled=True)

    normed_all = (norm_parts(whole_tokens.astype(F32))[0] * norms[0] + norms[1]).astype(BF16)
    qkv = dot(normed_all, whole_here).astype(BF16)
    mixed_heads, out_t, total = attend_forward(slot_of, place_of, qkv, heads)
    mixed = ctx_exchange(mixed_heads.reshape(ctx, rows, lanes), 2, sizes)
    mixed = mixed.transpose(1, 0, 2).reshape(rows, width)

    middle = start.astype(F32) + dot(mixed, whole_mixing)
    normal_two, inverse_two = norm_parts(middle)
    normed_two = (normal_two * norms[2] + norms[3]).astype(BF16)
    normed_two_all = fsdp_gather(normed_two, 3, sizes).reshape(fsdp * rows, width)
    expanded = dot(normed_two_all, expand_columns)
    grad_activated = (
        lax.dot_general(
            grads_in, w_shrink, (((1,), (1,)), ((), ())), preferred_element_type=F32
        )
        .astype(BF16)
        .astype(F32)
    )
    activated, slope = gelu_and_slope(expanded)
    activated = activated.astype(BF16)
    grad_expanded = (grad_activated * slope).astype(BF16)
    part_normed_two = lax.dot_general(
        grad_expanded, expand_columns, (((1,), (1,)), ((), ())), preferred_element_type=F32
    ).astype(BF16)
    part_out = dot(activated, w_shrink).astype(BF16)
    grad_normed_two = fsdp_scatter(part_normed_two.reshape(fsdp, rows, width), 4, sizes)
    layer_out = (
        middle + fsdp_scatter(part_out.reshape(fsdp, rows, width), 5, sizes)
    ).astype(BF16)
    grad_shrink = lax.dot_general(
        activated, grads_in, (((0,), (0,)), ((), ())), preferred_element_type=F32
    ).astype(BF16)
    grad_expand = lax.dot_general(
        normed_two_all, grad_expanded, (((0,), (0,)), ((), ())), preferred_element_type=F32
    ).astype(BF16)

    grad_middle = incoming.astype(F32) + norm_back(
        grad_normed_two, norms[2], normal_two, inverse_two
    )
    grad_branch = grad_middle.astype(BF16)
    grad_mixing = lax.dot_general(
        mixed, grad_branch, (((0,), (0,)), ((), ())), preferred_element_type=F32
    ).astype(BF16)
    grad_mixed = lax.dot_general(
        grad_branch, whole_mixing, (((1,), (1,)), ((), ())), preferred_element_type=F32
    ).astype(BF16)
    grad_heads = ctx_exchange(
        grad_mixed.reshape(rows, ctx, lanes).transpose(1, 0, 2), 2, sizes
    ).reshape(length, lanes)
    d_qkv = attend_backward(slot_of, place_of, qkv, grad_heads, out_t, total, heads)
    grad_joint = (
        ctx_exchange(d_qkv.reshape(ctx, rows, 3 * lanes), 6, sizes)
        .transpose(1, 0, 2)
        .reshape(rows, 3 * width)
    )
    grad_normed = lax.dot_general(
        grad_joint, whole_attend, (((1,), (1,)), ((), ())), preferred_element_type=F32
    )
    normal_one, inverse_one = norm_parts(start.astype(F32))
    tokens_grad = (
        grad_middle + norm_back(grad_normed, norms[0], normal_one, inverse_one)
    )[None]
    grad_norms = jnp.stack(
        [
            jnp.sum(grad_normed * normal_one, axis=0),
            jnp.sum(grad_normed, axis=0),
            jnp.sum(grad_normed_two * normal_two, axis=0),
            jnp.sum(grad_normed_two, axis=0),
        ]
    )
    sum_norms = lax.dynamic_slice_in_dim(
        lax.psum(grad_norms, ("fsdp", "ctx")), f * own, own, 1
    )

    part_attend = lax.dot_general(
        normed_all, d_qkv, (((0,), (0,)), ((), ())), preferred_element_type=F32
    ).astype(BF16)
    own_attend = fsdp_scatter(part_attend.reshape(fsdp, own, 3 * lanes), 7, sizes).astype(BF16)
    sum_attend = (
        lax.all_gather(own_attend, "ctx", axis=0, tiled=False)
        .reshape(ctx, own, 3, lanes)
        .transpose(1, 2, 0, 3)
        .reshape(own, 3 * width)
        .astype(F32)
    )

    own_mixing = lax.psum_scatter(grad_mixing, "fsdp", scatter_dimension=0, tiled=True)
    piece = own // ctx
    shrink_piece = hidden // ctx
    stacked = jnp.concatenate(
        [
            grad_shrink.reshape(ctx, shrink_piece, width),
            grad_expand.reshape(fsdp, ctx, piece, hidden)
            .transpose(1, 0, 2, 3)
            .reshape(ctx, fsdp * piece * hidden // width, width),
            own_mixing.reshape(ctx, piece, width),
        ],
        axis=1,
    )
    stacked = lax.psum_scatter(stacked, "ctx", scatter_dimension=0, tiled=False)
    expand_rows = fsdp * piece * hidden // width
    expand_piece = lax.all_to_all(
        stacked[shrink_piece : shrink_piece + expand_rows].reshape(fsdp, piece, hidden),
        "fsdp",
        split_axis=0,
        concat_axis=0,
        tiled=True,
    )
    expand_piece = expand_piece.transpose(1, 0, 2).reshape(expand_rows, width)
    stacked = jnp.concatenate(
        [stacked[:shrink_piece], expand_piece, stacked[shrink_piece + expand_rows :]], axis=0
    )
    stacked = lax.all_gather(stacked, "ctx", axis=0, tiled=False)
    sum_shrink = stacked[:, :shrink_piece].reshape(hidden, width).astype(F32)
    sum_expand = (
        stacked[:, shrink_piece : shrink_piece + expand_rows]
        .reshape(own, fsdp * hidden)
        .astype(F32)
    )
    sum_mixing = stacked[:, shrink_piece + expand_rows :].reshape(own, width).astype(F32)

    result = [layer_out[None], tokens_grad]
    for weight, grad, first, second in (
        (w_attend, sum_attend, first_attend, second_attend),
        (w_mixing, sum_mixing, first_mixing, second_mixing),
        (w_expand, sum_expand, first_expand, second_expand),
        (w_shrink, sum_shrink, first_shrink, second_shrink),
        (w_norms, sum_norms, first_norms, second_norms),
    ):
        result.append(grad)
        result.extend(adam_step(weight, grad, first, second))
    return tuple(result)


def solution(mesh):
    rows = P("fsdp", None)
    columns = P(None, "fsdp")
    tokens = P("fsdp", "ctx", None)
    return jax.shard_map(
        functools.partial(shards, (mesh.shape["fsdp"], mesh.shape["ctx"])),
        mesh=mesh,
        in_specs=(tokens, tokens, rows)
        + (rows, rows, rows, rows, columns) * 3,
        out_specs=(tokens, tokens) + (rows,) * 16 + (columns,) * 4,
        check_vma=False,
    )
```

```python
import functools
import math

import jax
import jax.numpy as jnp
from jax import lax
from jax.experimental import pallas as pl
from jax.experimental.pallas import tpu as pltpu
from jax.sharding import PartitionSpec as P

HD = 64
STEP_COUNT = 10
EPS_NORM = 1e-05
NEG = -1e30
BETA_ONE = 0.9
BETA_TWO = 0.999
LEARN = 0.02
DECAY = 0.1
EPS_ADAM = 1e-08
CUBIC = 0.044715
ROOT_TWO_PI = math.sqrt(2.0 / math.pi)
LOG2E = math.log2(math.e)
TILE = 256
MESH = pl.DeviceIdType.MESH
F32 = jnp.float32
BF16 = jnp.bfloat16


def dot(left, right):
    return jnp.dot(left, right, preferred_element_type=F32)


def norm_parts(values):
    center = values - jnp.mean(values, axis=-1, keepdims=True)
    spread = jnp.mean(center * center, axis=-1, keepdims=True)
    inverse = lax.rsqrt(spread + EPS_NORM)
    return center * inverse, inverse


def norm_back(err, gain, normal, inverse):
    scaled = err * gain
    first = jnp.mean(scaled, axis=-1, keepdims=True)
    second = jnp.mean(scaled * normal, axis=-1, keepdims=True)
    return inverse * (scaled - first - normal * second)


def gelu_and_slope(values):
    square = values * values
    inner = ROOT_TWO_PI * values * (1.0 + CUBIC * square)
    tanh = jnp.tanh(inner)
    half = 0.5 * (1.0 + tanh)
    slope = half + 0.5 * values * (1.0 - tanh * tanh) * ROOT_TWO_PI * (
        1.0 + 3.0 * CUBIC * square
    )
    return values * half, slope


def adam_step(weight, grad, first, second):
    first_new = BETA_ONE * first + (1.0 - BETA_ONE) * grad
    second_new = BETA_TWO * second + (1.0 - BETA_TWO) * grad * grad
    mean_hat = first_new / (1.0 - BETA_ONE**STEP_COUNT)
    square_hat = second_new / (1.0 - BETA_TWO**STEP_COUNT)
    update = -LEARN * (
        mean_hat / (jnp.sqrt(square_hat) + EPS_ADAM) + DECAY * weight.astype(F32)
    )
    return (update, first_new, second_new)


def comm_call(kernel, out_shape, scratch, ident, operands, any_space=True):
    space = pl.ANY if any_space else pltpu.VMEM
    outs = jax.tree.map(lambda _: pl.BlockSpec(memory_space=space), out_shape)
    return pl.pallas_call(
        kernel,
        out_shape=out_shape,
        in_specs=[pl.BlockSpec(memory_space=space)] * len(operands),
        out_specs=outs,
        scratch_shapes=scratch,
        compiler_params=pltpu.CompilerParams(collective_id=ident, has_side_effects=True),
    )(*operands)


def remote(src, dst, send, recv, device):
    return pltpu.make_async_remote_copy(
        src_ref=src,
        dst_ref=dst,
        send_sem=send,
        recv_sem=recv,
        device_id=device,
        device_id_type=MESH,
    )


def fsdp_partners():
    f, c = lax.axis_index("fsdp"), lax.axis_index("ctx")
    x, k = f // 2, f % 2
    return f, c, x, k, x * 2 + 1 - k, (1 - x) * 2 + k


def greet(devices):
    barrier = pltpu.get_barrier_semaphore()
    for device in devices:
        pl.semaphore_signal(barrier, inc=1, device_id=device, device_id_type=MESH)
    pl.semaphore_wait(barrier, len(devices))


CHUNKS = 4


class Pieces:
    def __init__(self, send_sems, recv_sems):
        self.send_sems, self.recv_sems, self.used = send_sems, recv_sems, 0

    def copy(self, src, dst, device):
        n = self.used
        self.used += 1
        return remote(src, dst, self.send_sems.at[n], self.recv_sems.at[n], device)


def row_parts(rows, count):
    step = rows // count
    return [pl.ds(t * step, step) for t in range(count)]


class FsdpGather:
    def __init__(self, pieces, x_ref, o_ref, local_sem, chunks=CHUNKS):
        f, c, x, k, mate, across = fsdp_partners()
        self.parts = row_parts(x_ref.shape[0], chunks)
        self.local = pltpu.make_async_copy(x_ref, o_ref.at[f], local_sem)
        self.far = [
            pieces.copy(x_ref.at[p], o_ref.at[f, p], (across, c)) for p in self.parts
        ]
        self.near = pieces.copy(x_ref, o_ref.at[f], (mate, c))
        self.passed = [
            pieces.copy(o_ref.at[across, p], o_ref.at[across, p], (mate, c))
            for p in self.parts
        ]

    def start(self):
        for copy in self.far:
            copy.start()
        self.near.start()
        self.local.start()

    def forward(self):
        for copy, onward in zip(self.far, self.passed):
            copy.wait_recv()
            onward.start()

    def finish(self):
        self.local.wait()
        self.near.wait()
        for copy, onward in zip(self.far, self.passed):
            copy.wait_send()
            onward.wait()


class FsdpScatter:
    def __init__(self, pieces, x_ref, near_buf, far_out, far_in, chunks=CHUNKS):
        f, c, x, k, mate, across = fsdp_partners()
        self.parts = row_parts(x_ref.shape[1], chunks)
        self.x_ref, self.near_buf, self.far_out, self.far_in = x_ref, near_buf, far_out, far_in
        self.f, self.across = f, across
        away_mate = (1 - x) * 2 + 1 - k
        self.near_far = [
            pieces.copy(x_ref.at[away_mate, p], near_buf.at[0, p], (mate, c))
            for p in self.parts
        ]
        self.near_own = pieces.copy(x_ref.at[mate], near_buf.at[1], (mate, c))
        self.far = [pieces.copy(far_out.at[p], far_in.at[p], (across, c)) for p in self.parts]

    def start(self):
        for copy in self.near_far:
            copy.start()
        self.near_own.start()

    def forward(self):
        for p, near, far in zip(self.parts, self.near_far, self.far):
            near.wait_recv()
            self.far_out[p] = (
                self.x_ref[self.across, p].astype(F32) + self.near_buf[0, p].astype(F32)
            ).astype(BF16)
            far.start()

    def finish(self, store):
        self.near_own.wait_recv()
        for p, far in zip(self.parts, self.far):
            far.wait_recv()
            store(
                p,
                self.x_ref[self.f, p].astype(F32)
                + self.near_buf[1, p].astype(F32)
                + self.far_in[p].astype(F32),
            )
        self.near_own.wait_send()
        for near, far in zip(self.near_far, self.far):
            near.wait_send()
            far.wait_send()


class CtxGather:
    def __init__(self, x_ref, o_ref, cut, local_sem, send_sem, recv_sem):
        f, c = lax.axis_index("fsdp"), lax.axis_index("ctx")
        self.f, self.c, self.z, self.y = f, c, c // 2, c % 2
        self.depth = o_ref.shape[0] // 2
        self.mate = self.z * 2 + 1 - self.y
        self.parts = (pl.ds(0, cut), pl.ds(cut, x_ref.shape[0] - cut))
        self.x_ref, self.o_ref, self.send_sem, self.recv_sem = x_ref, o_ref, send_sem, recv_sem
        self.local = pltpu.make_async_copy(x_ref, o_ref.at[c], local_sem)

    @staticmethod
    def semaphores(n):
        return [
            pltpu.SemaphoreType.DMA,
            pltpu.SemaphoreType.DMA((n, 2, 3)),
            pltpu.SemaphoreType.DMA((n, 2)),
        ]

    def copy(self, zz, yy, part, way, own=False):
        block = zz * 2 + yy
        src = self.x_ref.at[self.parts[part]] if own else self.o_ref.at[block, self.parts[part]]
        there = (self.c - 2, self.c + 2, self.mate)[way]
        return remote(
            src,
            self.o_ref.at[block, self.parts[part]],
            self.send_sem.at[block, part, way],
            self.recv_sem.at[block, part],
            (self.f, there),
        )

    def start(self):
        z, y = self.z, self.y
        self.local.start()
        for part in (0, 1):
            pl.when(z < self.depth - 1)(lambda: self.copy(z, y, part, 1, True).start())
            pl.when(z > 0)(lambda: self.copy(z, y, part, 0, True).start())
        for part in (1, 0):
            self.copy(z, y, part, 2, True).start()

    def arrive(self, zz, yy, part, way):
        self.copy(zz, yy, part, way).wait_recv()
        if way == 1:
            pl.when(self.z < self.depth - 1)(lambda: self.copy(zz, yy, part, 1).start())
        else:
            pl.when(self.z > 0)(lambda: self.copy(zz, yy, part, 0).start())
        if part == 0:
            self.copy(zz, yy, part, 2).start()

    def along(self, step, yy, part):
        z = self.z
        pl.when(z - step >= 0)(lambda: self.arrive(z - step, yy, part, 1))
        pl.when(z + step < self.depth)(lambda: self.arrive(z + step, yy, part, 0))

    def forward(self):
        z, y = self.z, self.y
        self.local.wait()
        for step in range(1, self.depth):
            self.along(step, y, 0)
            self.along(step, y, 1)
            if step == 1:
                self.copy(z, 1 - y, 1, 2).wait_recv()
                pl.when(z < self.depth - 1)(lambda: self.copy(z, 1 - y, 1, 1).start())
                pl.when(z > 0)(lambda: self.copy(z, 1 - y, 1, 0).start())
            self.along(step, 1 - y, 1)

    def finish(self):
        z, y, depth = self.z, self.y, self.depth
        self.copy(z, 1 - y, 0, 2).wait_recv()
        for step in range(1, depth):
            pl.when(z - step >= 0)(lambda: self.copy(z - step, 1 - y, 0, 2).wait_recv())
            pl.when(z + step < depth)(lambda: self.copy(z + step, 1 - y, 0, 2).wait_recv())
        for step in range(depth):
            for yy, part in ((y, 0), (y, 1), (1 - y, 1)):

                def sent_right():
                    self.copy(z - step, yy, part, 1).wait_send()

                def sent_left():
                    self.copy(z + step, yy, part, 0).wait_send()

                pl.when((z - step >= 0) & (z < depth - 1))(sent_right)
                pl.when((z + step < depth) & (z > 0))(sent_left)
        self.copy(z, y, 0, 2).wait_send()
        self.copy(z, y, 1, 2).wait_send()
        for step in range(1, depth):
            pl.when(z - step >= 0)(lambda: self.copy(z - step, y, 0, 2).wait_send())
            pl.when(z + step < depth)(lambda: self.copy(z + step, y, 0, 2).wait_send())


def greet_lines(others, depth):
    f, c = lax.axis_index("fsdp"), lax.axis_index("ctx")
    z = c // 2
    barrier = pltpu.get_barrier_semaphore()

    def signal(device):
        pl.semaphore_signal(barrier, inc=1, device_id=device, device_id_type=MESH)

    for device in others:
        signal(device)
    pl.when(z > 0)(lambda: signal((f, c - 2)))
    pl.when(z < depth - 1)(lambda: signal((f, c + 2)))
    pl.semaphore_wait(
        barrier, len(others) + (z + depth - 1) // depth + (2 * depth - 2 - z) // depth
    )


def gather_cut(rows):
    return rows * 13 // 16 // 8 * 8


def start_kernel(
    tokens_ref, attend_ref, norms_ref, expand_ref,
    tokens_out, attend_out, norms_out, expand_out,
    local_sems, send_sems, recv_sems, ctx_local, ctx_send, ctx_recv,
):
    f, c, x, k, mate, across = fsdp_partners()
    n = tokens_out.shape[0]
    others = [(f + j) % 4 for j in (1, 2, 3)]
    greet_lines([(o, c) for o in others] + [(f, c // 2 * 2 + 1 - c % 2)], n // 2)
    pieces = Pieces(send_sems, recv_sems)
    tokens = CtxGather(
        tokens_ref, tokens_out, gather_cut(tokens_ref.shape[0]), ctx_local, ctx_send, ctx_recv
    )
    tokens.start()
    attend = FsdpGather(pieces, attend_ref, attend_out, local_sems.at[0], 2)
    attend.start()
    own, hidden = expand_ref.shape[0], expand_out.shape[1]
    copies = [pieces.copy(norms_ref, norms_out.at[f], (o, c)) for o in others]
    for o in others:
        copies.append(
            pieces.copy(
                expand_ref.at[:, pl.ds(pl.multiple_of(o * hidden, 128), hidden)],
                expand_out.at[pl.ds(pl.multiple_of(f * own, 16), own)],
                (o, c),
            )
        )
    for copy in copies:
        copy.start()
    stay = [
        pltpu.make_async_copy(norms_ref, norms_out.at[f], local_sems.at[1]),
        pltpu.make_async_copy(
            expand_ref.at[:, pl.ds(pl.multiple_of(f * hidden, 128), hidden)],
            expand_out.at[pl.ds(pl.multiple_of(f * own, 16), own)],
            local_sems.at[2],
        ),
    ]
    for copy in stay:
        copy.start()
    attend.forward()
    tokens.forward()
    attend.finish()
    for copy in copies + stay:
        copy.wait()
    tokens.finish()


def start_exchange(tokens, attend_here, norms, w_expand, hidden, sizes):
    fsdp, ctx = sizes
    if sizes != (4, 8):
        own = w_expand.shape[0]
        columns = lax.all_to_all(
            w_expand.reshape(own, fsdp, hidden).transpose(1, 0, 2),
            "fsdp",
            split_axis=0,
            concat_axis=0,
            tiled=True,
        )
        return (
            lax.all_gather(tokens, "ctx", axis=0, tiled=False),
            lax.all_gather(attend_here, "fsdp", axis=0, tiled=False),
            lax.all_gather(norms, "fsdp", axis=0, tiled=False),
            columns.reshape(fsdp * own, hidden),
        )
    return comm_call(
        start_kernel,
        (
            jax.ShapeDtypeStruct((ctx,) + tokens.shape, BF16),
            jax.ShapeDtypeStruct((fsdp,) + attend_here.shape, BF16),
            jax.ShapeDtypeStruct((fsdp,) + norms.shape, F32),
            jax.ShapeDtypeStruct((fsdp * w_expand.shape[0], hidden), BF16),
        ),
        [
            pltpu.SemaphoreType.DMA((3,)),
            pltpu.SemaphoreType.DMA((11,)),
            pltpu.SemaphoreType.DMA((11,)),
        ]
        + CtxGather.semaphores(ctx),
        0,
        (tokens, attend_here, norms, w_expand),
    )


def fsdp_gather_kernel(x_ref, o_ref, local_sem, send_sems, recv_sems):
    f, c, x, k, mate, across = fsdp_partners()
    greet([(mate, c), (across, c)])
    gather = FsdpGather(Pieces(send_sems, recv_sems), x_ref, o_ref, local_sem)
    gather.start()
    gather.forward()
    gather.finish()


def fsdp_gather(values, ident, sizes):
    if sizes != (4, 8):
        return lax.all_gather(values, "fsdp", axis=0, tiled=False)
    return comm_call(
        fsdp_gather_kernel,
        jax.ShapeDtypeStruct((4,) + values.shape, values.dtype),
        [
            pltpu.SemaphoreType.DMA,
            pltpu.SemaphoreType.DMA((2 * CHUNKS + 1,)),
            pltpu.SemaphoreType.DMA((2 * CHUNKS + 1,)),
        ],
        ident,
        (values,),
    )


def scatter_buffers(rows, width):
    return [
        pltpu.VMEM((2, rows, width), BF16),
        pltpu.VMEM((rows, width), BF16),
        pltpu.VMEM((rows, width), BF16),
    ]


def fsdp_scatter_kernel(x_ref, o_ref, near_buf, far_out, far_in, send_sems, recv_sems):
    f, c, x, k, mate, across = fsdp_partners()
    greet([(mate, c), (across, c)])
    scatter = FsdpScatter(Pieces(send_sems, recv_sems), x_ref, near_buf, far_out, far_in)
    scatter.start()
    scatter.forward()

    def store(p, value):
        o_ref[p] = value

    scatter.finish(store)


def fsdp_scatter(values, ident, sizes):
    if sizes != (4, 8):
        return lax.psum_scatter(values, "fsdp", scatter_dimension=0, tiled=False).astype(F32)
    rows, width = values.shape[1:]
    return comm_call(
        fsdp_scatter_kernel,
        jax.ShapeDtypeStruct((rows, width), F32),
        scatter_buffers(rows, width)
        + [
            pltpu.SemaphoreType.DMA((2 * CHUNKS + 1,)),
            pltpu.SemaphoreType.DMA((2 * CHUNKS + 1,)),
        ],
        ident,
        (values,),
        any_space=False,
    )


class CtxExchange:
    def __init__(self, pieces, n, source, target, local_sem):
        f, c = lax.axis_index("fsdp"), lax.axis_index("ctx")
        self.copies = []
        for j in range(n - 1, 0, -1):
            there = (c + j) % n
            self.copies.append(pieces.copy(source(there), target(c), (f, there)))
        self.local = pltpu.make_async_copy(source(c), target(c), local_sem)

    def start(self):
        for copy in self.copies:
            copy.start()
        self.local.start()

    def finish(self):
        self.local.wait()
        for copy in self.copies:
            copy.wait()


def greet_ctx(n, others=()):
    f, c = lax.axis_index("fsdp"), lax.axis_index("ctx")
    greet([(f, (c + j) % n) for j in range(1, n)] + list(others))


def column_block(ref, block, lanes):
    return ref.at[:, pl.ds(pl.multiple_of(block * lanes, 128), lanes)]


def ctx_to_rows_kernel(n, x_ref, o_ref, local_sem, send_sems, recv_sems):
    lanes = x_ref.shape[-1]
    greet_ctx(n)
    move = CtxExchange(
        Pieces(send_sems, recv_sems),
        n,
        lambda j: x_ref.at[j],
        lambda j: column_block(o_ref, j, lanes),
        local_sem,
    )
    move.start()
    move.finish()


def ctx_to_heads_kernel(n, x_ref, o_ref, local_sem, send_sems, recv_sems):
    lanes = o_ref.shape[-1]
    greet_ctx(n)
    move = CtxExchange(
        Pieces(send_sems, recv_sems),
        n,
        lambda j: column_block(x_ref, j, lanes),
        lambda j: o_ref.at[j],
        local_sem,
    )
    move.start()
    move.finish()


def exchange_semaphores(n):
    return [
        pltpu.SemaphoreType.DMA,
        pltpu.SemaphoreType.DMA((n - 1,)),
        pltpu.SemaphoreType.DMA((n - 1,)),
    ]


def ctx_to_rows(values, ident, sizes):
    n, rows, lanes = values.shape
    if sizes != (4, 8):
        moved = lax.all_to_all(values, "ctx", split_axis=0, concat_axis=0, tiled=True)
        return moved.transpose(1, 0, 2).reshape(rows, n * lanes)
    return comm_call(
        functools.partial(ctx_to_rows_kernel, n),
        jax.ShapeDtypeStruct((rows, n * lanes), values.dtype),
        exchange_semaphores(n),
        ident,
        (values,),
    )


def ctx_to_heads(values, ident, sizes):
    n = sizes[1]
    rows, lanes = values.shape[0], values.shape[1] // n
    if sizes != (4, 8):
        return lax.all_to_all(
            values.reshape(rows, n, lanes).transpose(1, 0, 2),
            "ctx",
            split_axis=0,
            concat_axis=0,
            tiled=True,
        )
    return comm_call(
        functools.partial(ctx_to_heads_kernel, n),
        jax.ShapeDtypeStruct((n, rows, lanes), values.dtype),
        exchange_semaphores(n),
        ident,
        (values,),
    )


def last_kernel(
    n, attend_ref, mixing_ref, norms_ref, shrink_ref, expand_ref,
    attend_out, mixing_out, norms_out, shrink_out, expand_out,
    near_buf, far_out, far_in, mixing_in, norms_in, norms_own, block, blocks, expand_own,
    send_sems, recv_sems, local_sems, *gather_sems,
):
    f, c, x, k, mate, across = fsdp_partners()
    lanes = mixing_in.shape[-1]
    wide = attend_ref.shape[-1]
    own = attend_ref.shape[1]
    hidden = expand_ref.shape[-1]
    others = [(f + j) % 4 for j in (1, 2, 3)]
    greet_ctx(n, [(o, c) for o in others])
    pieces = Pieces(send_sems, recv_sems)
    sems = [gather_sems[3 * j : 3 * j + 3] for j in range(4)]

    def columns(j):
        return expand_own.at[:, pl.ds(pl.multiple_of(j * hidden, 128), hidden)]

    scatter = FsdpScatter(pieces, attend_ref, near_buf, far_out, far_in, 2)
    scatter.start()
    early = [pieces.copy(norms_ref.at[o], norms_in.at[f], (o, c)) for o in others]
    early += [pieces.copy(expand_ref.at[o], columns(f), (o, c)) for o in others]
    move = CtxExchange(
        pieces,
        n,
        lambda j: column_block(mixing_ref, j, lanes),
        lambda j: mixing_in.at[j],
        local_sems.at[0],
    )
    early += [
        pltpu.make_async_copy(norms_ref.at[f], norms_in.at[f], local_sems.at[1]),
        pltpu.make_async_copy(expand_ref.at[f], columns(f), local_sems.at[2]),
    ]
    for copy in early:
        copy.start()
    move.start()
    shrink = CtxGather(shrink_ref, shrink_out, gather_cut(shrink_ref.shape[0]), *sems[0])
    shrink.start()
    scatter.forward()
    for copy in early:
        copy.wait()
    norms_own[...] = norms_in[0] + norms_in[1] + norms_in[2] + norms_in[3]
    expand = CtxGather(expand_own, expand_out, gather_cut(expand_own.shape[0]), *sems[1])
    small = CtxGather(norms_own, norms_out, 4, *sems[2])
    expand.start()
    small.start()
    move.finish()
    total = mixing_in[0].astype(F32)
    for j in range(1, n):
        total += mixing_in[j].astype(F32)
    block[:, wide:] = total.astype(BF16)

    def store(p, value):
        block[p, :wide] = value.astype(BF16)

    scatter.finish(store)
    gather = CtxGather(block, blocks, gather_cut(own), *sems[3])
    gather.start()
    for each in (shrink, expand, small, gather):
        each.forward()
    for each in (shrink, expand, small, gather):
        each.finish()
    for j in range(n):
        for part in range(3):
            at = (part * n + j) * lanes
            attend_out[:, at : at + lanes] = blocks[j, :, part * lanes : (part + 1) * lanes]
        mixing_out[:, j * lanes : (j + 1) * lanes] = blocks[j, :, wide:]


def last_exchange(part_attend, own_mixing, grad_norms, shrink_piece, expand_piece, sizes):
    fsdp, n = sizes
    own, wide = part_attend.shape[1:]
    width = own_mixing.shape[1]
    lanes = width // n
    _, piece, hidden = expand_piece.shape
    if sizes != (4, 8):
        own_attend = lax.psum_scatter(part_attend, "fsdp", scatter_dimension=0, tiled=False)
        attend = (
            lax.all_gather(own_attend, "ctx", axis=0, tiled=False)
            .reshape(n, own, 3, lanes)
            .transpose(1, 2, 0, 3)
            .reshape(own, 3 * width)
        )
        norms = lax.psum_scatter(grad_norms, "fsdp", scatter_dimension=0, tiled=False)
        expand = lax.all_to_all(expand_piece, "fsdp", split_axis=0, concat_axis=0, tiled=True)
        expand = expand.transpose(1, 0, 2).reshape(piece, fsdp * hidden)
        return (
            attend,
            lax.psum(own_mixing, "ctx"),
            lax.all_gather(norms, "ctx", axis=0, tiled=False),
            lax.all_gather(shrink_piece, "ctx", axis=0, tiled=True),
            lax.all_gather(expand, "ctx", axis=0, tiled=True),
        )
    count = 2 * 2 + 1 + n - 1 + 6
    vmem, anywhere = pl.BlockSpec(memory_space=pltpu.VMEM), pl.BlockSpec(memory_space=pl.ANY)
    attend, mixing, norms, shrink, expand = pl.pallas_call(
        functools.partial(last_kernel, n),
        out_shape=(
            jax.ShapeDtypeStruct((own, 3 * width), BF16),
            jax.ShapeDtypeStruct((own, width), BF16),
            jax.ShapeDtypeStruct((n,) + grad_norms.shape[1:], F32),
            jax.ShapeDtypeStruct((n,) + shrink_piece.shape, BF16),
            jax.ShapeDtypeStruct((n, piece, fsdp * hidden), BF16),
        ),
        in_specs=[vmem, vmem, vmem, anywhere, anywhere],
        out_specs=(vmem, vmem, vmem, anywhere, anywhere),
        scratch_shapes=scatter_buffers(own, wide)
        + [
            pltpu.VMEM((n, own, lanes), BF16),
            pltpu.VMEM(grad_norms.shape, F32),
            pltpu.VMEM(grad_norms.shape[1:], F32),
            pltpu.VMEM((own, wide + lanes), BF16),
            pltpu.VMEM((n, own, wide + lanes), BF16),
            pltpu.VMEM((piece, fsdp * hidden), BF16),
            pltpu.SemaphoreType.DMA((count,)),
            pltpu.SemaphoreType.DMA((count,)),
            pltpu.SemaphoreType.DMA((3,)),
        ]
        + CtxGather.semaphores(n) * 4,
        compiler_params=pltpu.CompilerParams(collective_id=7, has_side_effects=True),
    )(part_attend, own_mixing, grad_norms, shrink_piece, expand_piece)
    return (
        attend,
        mixing,
        norms,
        shrink.reshape(n * shrink_piece.shape[0], width),
        expand.reshape(n * piece, fsdp * hidden),
    )


def head_rows(h):
    return slice(h * HD, (h + 1) * HD)


def attend_forward_kernel(
    heads, slot_ref, place_ref, qkv_ref, mixed_ref, out_t_ref, total_ref,
    q_pos, k_pos, v_pos, q_t, v_t, scores, o_pos,
):
    length, lanes = q_pos.shape
    blocks = slot_ref.shape[0]
    size = length // blocks
    tiles = length // TILE
    factor = LOG2E / math.sqrt(HD)
    for p in range(blocks):
        rows = qkv_ref[pl.ds(slot_ref[p] * size, size), :]
        here = slice(p * size, (p + 1) * size)
        q_pos[here, :] = rows[:, :lanes]
        k_pos[here, :] = rows[:, lanes : 2 * lanes]
        v_pos[here, :] = rows[:, 2 * lanes :]
    for t in range(tiles):
        here = slice(t * TILE, (t + 1) * TILE)
        q_t[:, here] = q_pos[here, :].T
        v_t[:, here] = v_pos[here, :].T
    head_of_row = lax.broadcasted_iota(jnp.int32, (lanes, TILE), 0) // HD
    allowed = lax.broadcasted_iota(jnp.int32, (TILE, TILE), 0) <= lax.broadcasted_iota(
        jnp.int32, (TILE, TILE), 1
    )

    def fold_max(values):
        return jnp.max(values.reshape(TILE // 8, 8, TILE), axis=0)

    def fold_sum(values):
        return jnp.sum(values.reshape(TILE // 8, 8, TILE), axis=0)

    @pl.loop(0, tiles)
    def _(i):
        here = pl.ds(pl.multiple_of(i * TILE, TILE), TILE)
        q_tile = q_t[:, here]
        q_heads = [
            jnp.where(head_of_row == h, q_tile, jnp.zeros_like(q_tile)) for h in range(heads)
        ]

        def first(j, tops):
            there = pl.ds(pl.multiple_of(j * TILE, TILE), TILE)
            keys = k_pos[there, :]
            result = []
            for h in range(heads):
                raw = dot(keys, q_heads[h])
                scores[h, there, :] = raw
                result.append(jnp.maximum(tops[h], fold_max(raw)))
            return tuple(result)

        tops = lax.fori_loop(
            0, i, first, tuple(jnp.full((8, TILE), NEG, F32) for _ in range(heads))
        )
        keys = k_pos[here, :]
        row_tops = []
        for h in range(heads):
            raw = jnp.where(allowed, dot(keys, q_heads[h]), NEG)
            scores[h, here, :] = raw
            row_tops.append(
                jnp.max(jnp.maximum(tops[h], fold_max(raw)), axis=0, keepdims=True) * factor
            )

        def second(j, state):
            there = pl.ds(pl.multiple_of(j * TILE, TILE), TILE)
            result = []
            for h in range(heads):
                sums, acc = state[h]
                probs = jnp.exp2(scores[h, there, :] * factor - row_tops[h])
                acc = acc + dot(v_t[head_rows(h), there], probs.astype(BF16))
                result.append((sums + fold_sum(probs), acc))
            return tuple(result)

        state = lax.fori_loop(
            0,
            i + 1,
            second,
            tuple(
                (jnp.zeros((8, TILE), F32), jnp.zeros((HD, TILE), F32)) for _ in range(heads)
            ),
        )
        outs = []
        for h in range(heads):
            sums, acc = state[h]
            row_sum = jnp.sum(sums, axis=0, keepdims=True)
            out = acc * (1.0 / row_sum)
            out_t_ref[head_rows(h), here] = out
            total_ref[pl.ds(h, 1), here] = row_tops[h] + jnp.log2(row_sum)
            outs.append(out)
        out = jnp.concatenate(outs, axis=0) if heads > 1 else outs[0]
        o_pos[here, :] = out.T.astype(BF16)

    for s in range(blocks):
        mixed_ref[s * size : (s + 1) * size, :] = o_pos[
            pl.ds(place_ref[s] * size, size), :
        ]


def attend_forward(slot_of, place_of, qkv, heads):
    length = qkv.shape[0]
    lanes = heads * HD
    vmem = pl.BlockSpec(memory_space=pltpu.VMEM)
    smem = pl.BlockSpec(memory_space=pltpu.SMEM)
    return pl.pallas_call(
        functools.partial(attend_forward_kernel, heads),
        out_shape=(
            jax.ShapeDtypeStruct((length, lanes), BF16),
            jax.ShapeDtypeStruct((lanes, length), F32),
            jax.ShapeDtypeStruct((8, length), F32),
        ),
        in_specs=[smem, smem, vmem],
        out_specs=(vmem, vmem, vmem),
        scratch_shapes=[pltpu.VMEM((length, lanes), BF16)] * 3
        + [pltpu.VMEM((lanes, length), BF16)] * 2
        + [pltpu.VMEM((heads, length, TILE), F32), pltpu.VMEM((length, lanes), BF16)],
        cost_estimate=pl.CostEstimate(
            flops=4 * length * length * lanes,
            bytes_accessed=10 * length * lanes,
            transcendentals=heads * length * length // 2,
        ),
    )(slot_of, place_of, qkv)


def attend_backward_kernel(
    heads, between, slot_ref, place_ref, qkv_ref, load_grad, out_t_ref, total_ref, result_ref,
    q_pos, k_pos, v_pos, g_pos, k_heads, v_heads, q_t, k_t, g_t, delta,
    dq_t, dk_acc, dv_acc, d_pos,
):
    length, lanes = q_pos.shape
    blocks = slot_ref.shape[0]
    size = length // blocks
    tiles = length // TILE
    scale = 1.0 / math.sqrt(HD)
    factor = LOG2E * scale
    for p in range(blocks):
        rows = qkv_ref[pl.ds(slot_ref[p] * size, size), :]
        here = slice(p * size, (p + 1) * size)
        q_pos[here, :] = rows[:, :lanes]
        k_pos[here, :] = rows[:, lanes : 2 * lanes]
        v_pos[here, :] = rows[:, 2 * lanes :]
    head_of_lane = lax.broadcasted_iota(jnp.int32, (TILE, lanes), 1) // HD
    allowed = lax.broadcasted_iota(jnp.int32, (TILE, TILE), 0) <= lax.broadcasted_iota(
        jnp.int32, (TILE, TILE), 1
    )
    for t in range(tiles):
        here = slice(t * TILE, (t + 1) * TILE)
        q_t[:, here] = q_pos[here, :].T
        k_t[:, here] = k_pos[here, :].T
        keys, values = k_pos[here, :], v_pos[here, :]
        for h in range(heads):
            k_heads[h, here, :] = jnp.where(head_of_lane == h, keys, jnp.zeros_like(keys))
            v_heads[h, here, :] = jnp.where(head_of_lane == h, values, jnp.zeros_like(values))
    dq_t[...] = jnp.zeros_like(dq_t)
    load = load_grad()
    for p in range(blocks):
        g_pos[p * size : (p + 1) * size, :] = load(slot_ref[p] * size, size)
    for t in range(tiles):
        here = slice(t * TILE, (t + 1) * TILE)
        g_tile = g_pos[here, :].T
        g_t[:, here] = g_tile
        product = g_tile.astype(F32) * out_t_ref[:, here]
        for h in range(heads):
            delta[h : h + 1, here] = jnp.sum(product[head_rows(h)], axis=0, keepdims=True)

    def pair(j, i, masked):
        there = pl.ds(pl.multiple_of(j * TILE, TILE), TILE)
        here = pl.ds(pl.multiple_of(i * TILE, TILE), TILE)
        for h in range(heads):
            raw = dot(k_heads[h, there, :], q_t[:, here])
            probs = jnp.exp2(raw * factor - total_ref[pl.ds(h, 1), here])
            if masked:
                probs = jnp.where(allowed, probs, 0.0)
            d_probs = dot(v_heads[h, there, :], g_t[:, here])
            d_scores = (probs * (d_probs - delta[pl.ds(h, 1), here])).astype(BF16)
            dv = dot(probs.astype(BF16), g_pos[here, :])
            dk = dot(d_scores, q_pos[here, :])
            if masked:
                dv_acc[h], dk_acc[h] = dv, dk
            else:
                dv_acc[h] += dv
                dk_acc[h] += dk
            dq_t[head_rows(h), here] += dot(k_t[head_rows(h), there], d_scores)

    @pl.loop(0, tiles)
    def _(j):
        pair(j, j, True)

        @pl.loop(j + 1, tiles)
        def _(i):
            pair(j, i, False)

        there = pl.ds(pl.multiple_of(j * TILE, TILE), TILE)
        for index, acc, weight in ((1, dk_acc, scale), (2, dv_acc, 1.0)):
            value = acc[0]
            for h in range(1, heads):
                value = jnp.where(head_of_lane == h, acc[h], value)
            d_pos[there, index * lanes : (index + 1) * lanes] = (value * weight).astype(BF16)
        between(j)

    for t in range(tiles):
        here = slice(t * TILE, (t + 1) * TILE)
        d_pos[here, :lanes] = (dq_t[:, here].T * scale).astype(BF16)
    for s in range(blocks):
        result_ref[s * size : (s + 1) * size, :] = d_pos[pl.ds(place_ref[s] * size, size), :]


def attend_backward_scratch(length, heads):
    lanes = heads * HD
    rows = pltpu.VMEM((length, lanes), BF16)
    columns = pltpu.VMEM((lanes, length), BF16)
    by_head = pltpu.VMEM((heads, length, lanes), BF16)
    return (
        [rows] * 4
        + [by_head] * 2
        + [columns] * 3
        + [
            pltpu.VMEM((8, length), F32),
            pltpu.VMEM((lanes, length), F32),
            pltpu.VMEM((heads, TILE, lanes), F32),
            pltpu.VMEM((heads, TILE, lanes), F32),
            pltpu.VMEM((length, 3 * lanes), BF16),
        ]
    )


ATTEND_SCRATCH = 14


def local_backward_kernel(
    heads, slot_ref, place_ref, qkv_ref, grad_ref, out_t_ref, total_ref, result_ref, *scratch
):
    attend_backward_kernel(
        heads, lambda j: None, slot_ref, place_ref, qkv_ref,
        lambda: lambda at, size: grad_ref[pl.ds(at, size), :],
        out_t_ref, total_ref, result_ref, *scratch,
    )


def attend_backward(slot_of, place_of, qkv, grad, out_t, total, heads):
    length = qkv.shape[0]
    lanes = heads * HD
    vmem = pl.BlockSpec(memory_space=pltpu.VMEM)
    smem = pl.BlockSpec(memory_space=pltpu.SMEM)
    return pl.pallas_call(
        functools.partial(local_backward_kernel, heads),
        out_shape=jax.ShapeDtypeStruct((length, 3 * lanes), BF16),
        in_specs=[smem, smem, vmem, vmem, vmem, vmem],
        out_specs=vmem,
        scratch_shapes=attend_backward_scratch(length, heads),
    )(slot_of, place_of, qkv, grad, out_t, total)


def backward_kernel(
    n, heads, slot_ref, place_ref, qkv_ref, out_t_ref, total_ref,
    mixed_ref, mixing_ref, out_ref, shrink_ref, expand_ref,
    result_ref, joint_ref, own_ref, branch_ref, piece_ref, *rest,
):
    scratch, rest = rest[:ATTEND_SCRATCH], rest[ATTEND_SCRATCH:]
    (
        grad_in, near_a, far_out_a, far_in_a, near_b, far_out_b, far_in_b,
        pair_in, pair_sum, line_in, local_sems, send_sems, recv_sems,
        pair_send, pair_recv, line_send, line_recv,
    ) = rest
    f, c, x, k, mate, across = fsdp_partners()
    depth = n // 2
    z, y = c // 2, c % 2
    lanes = heads * HD
    half = shrink_ref.shape[1]
    fsdp, _, small, hidden = expand_ref.shape
    length = qkv_ref.shape[0]
    rows = length // n
    greet_ctx(n, [(mate, c), (across, c)])
    pieces = Pieces(send_sems, recv_sems)
    to_heads = CtxExchange(
        pieces, n, lambda j: column_block(mixed_ref, j, lanes), lambda j: grad_in.at[j],
        local_sems.at[0],
    )
    to_rows = CtxExchange(
        pieces, n, lambda j: result_ref.at[pl.ds(pl.multiple_of(j * rows, 128), rows)],
        lambda j: column_block(joint_ref, j, 3 * lanes), local_sems.at[1],
    )
    mixing = FsdpScatter(pieces, mixing_ref, near_a, far_out_a, far_in_a)
    branch = FsdpScatter(pieces, out_ref, near_b, far_out_b, far_in_b)
    to_heads.start()

    def pair_copies(t):
        to = (z + 1 + t) % depth * 2 + 1 - y
        there = (f, z * 2 + 1 - y)
        return [
            remote(
                shrink_ref.at[to], pair_in.at[t, pl.ds(0, half)],
                pair_send.at[t, 0], pair_recv.at[t, 0], there,
            )
        ] + [
            remote(
                expand_ref.at[j, to], pair_in.at[t, pl.ds(half + j * small, small)],
                pair_send.at[t, 1 + j], pair_recv.at[t, 1 + j], there,
            )
            for j in range(fsdp)
        ]

    def pair_total(t):
        for copy in pair_copies(t):
            copy.wait_recv()
        to = (z + 1 + t) % depth * 2 + y
        yield 0, half, shrink_ref[to].astype(F32) + pair_in[t, :half].astype(F32)
        for j in range(fsdp):
            at = half + j * small
            yield at, small, (
                expand_ref[j, to].astype(F32) + pair_in[t, at : at + small].astype(F32)
            )

    def line_copy(t):
        return remote(
            pair_sum.at[t], line_in.at[t], line_send.at[t], line_recv.at[t],
            (f, (z + 1 + t) % depth * 2 + y),
        )

    for t in range(depth):
        for copy in pair_copies(t):
            copy.start()
    mixing.start()
    mixing.forward()
    branch.start()
    branch.forward()

    def load_grad():
        to_heads.finish()

        def load(at, size):
            return grad_in[at // rows, pl.ds(at % rows, size), :]

        return load

    def between(j):
        @pl.when((j % 2 == 0) & (j < 2 * (depth - 1)))
        def _():
            t = j // 2
            for at, count, value in pair_total(t):
                pair_sum[t, at : at + count] = value.astype(BF16)
            line_copy(t).start()

    attend_backward_kernel(
        heads, between, slot_ref, place_ref, qkv_ref, load_grad, out_t_ref, total_ref,
        result_ref, *scratch,
    )
    to_rows.start()

    def store_own(p, value):
        own_ref[p] = value.astype(BF16)

    def store_branch(p, value):
        branch_ref[p] = value

    mixing.finish(store_own)
    branch.finish(store_branch)
    for t in range(depth - 1):
        line_copy(t).wait_recv()
    for at, count, value in pair_total(depth - 1):
        for t in range(depth - 1):
            value += line_in[t, at : at + count].astype(F32)
        piece_ref[at : at + count] = value.astype(BF16)
    for t in range(depth):
        for copy in pair_copies(t):
            copy.wait_send()
    for t in range(depth - 1):
        line_copy(t).wait_send()
    to_rows.finish()


def backward_exchange(
    slot_of, place_of, qkv, out_t, total, grad_mixed, grad_mixing, part_out,
    grad_shrink, grad_expand, heads, sizes,
):
    fsdp, n = sizes
    length = qkv.shape[0]
    rows, lanes = length // n, heads * HD
    width = grad_mixed.shape[1]
    own = width // fsdp
    hidden = grad_expand.shape[1]
    small = own // n
    if sizes != (4, 8):
        grad_heads = ctx_to_heads(grad_mixed, None, sizes).reshape(length, lanes)
        d_qkv = attend_backward(slot_of, place_of, qkv, grad_heads, out_t, total, heads)
        shrink = lax.psum_scatter(grad_shrink, "ctx", scatter_dimension=0, tiled=True)
        expand = lax.psum_scatter(
            grad_expand.reshape(fsdp, n, small, hidden)
            .transpose(1, 0, 2, 3)
            .reshape(n * fsdp * small, hidden),
            "ctx",
            scatter_dimension=0,
            tiled=True,
        )
        return (
            d_qkv,
            ctx_to_rows(d_qkv.reshape(n, rows, 3 * lanes), None, sizes),
            lax.psum_scatter(grad_mixing, "fsdp", scatter_dimension=0, tiled=True),
            lax.psum_scatter(part_out, "fsdp", scatter_dimension=0, tiled=True).astype(F32),
            shrink,
            expand.reshape(fsdp, small, hidden),
        )
    half = hidden // n
    tall = half + fsdp * small
    depth = n // 2
    count = 2 * (n - 1) + 2 * (2 * CHUNKS + 1)
    vmem, anywhere = pl.BlockSpec(memory_space=pltpu.VMEM), pl.BlockSpec(memory_space=pl.ANY)
    smem = pl.BlockSpec(memory_space=pltpu.SMEM)
    d_qkv, joint, own_mixing, branch, piece = pl.pallas_call(
        functools.partial(backward_kernel, n, heads),
        out_shape=(
            jax.ShapeDtypeStruct((length, 3 * lanes), BF16),
            jax.ShapeDtypeStruct((rows, 3 * width), BF16),
            jax.ShapeDtypeStruct((own, width), BF16),
            jax.ShapeDtypeStruct((rows, width), F32),
            jax.ShapeDtypeStruct((tall, width), BF16),
        ),
        in_specs=[smem, smem] + [vmem] * 8,
        out_specs=(vmem, anywhere, vmem, vmem, vmem),
        scratch_shapes=attend_backward_scratch(length, heads)
        + [pltpu.VMEM((n, rows, lanes), BF16)]
        + scatter_buffers(own, width)
        + scatter_buffers(rows, width)
        + [
            pltpu.VMEM((depth, tall, width), BF16),
            pltpu.VMEM((depth - 1, tall, width), BF16),
            pltpu.VMEM((depth - 1, tall, width), BF16),
            pltpu.SemaphoreType.DMA((2,)),
            pltpu.SemaphoreType.DMA((count,)),
            pltpu.SemaphoreType.DMA((count,)),
            pltpu.SemaphoreType.DMA((depth, 1 + fsdp)),
            pltpu.SemaphoreType.DMA((depth, 1 + fsdp)),
            pltpu.SemaphoreType.DMA((depth - 1,)),
            pltpu.SemaphoreType.DMA((depth - 1,)),
        ],
        compiler_params=pltpu.CompilerParams(
            collective_id=6, has_side_effects=True, vmem_limit_bytes=58 * 2**20
        ),
    )(
        slot_of,
        place_of,
        qkv,
        out_t,
        total,
        grad_mixed,
        grad_mixing.reshape(fsdp, own, width),
        part_out.reshape(fsdp, rows, width),
        grad_shrink.reshape(n, half, width),
        grad_expand.reshape(fsdp, n, small, hidden),
    )
    return d_qkv, joint, own_mixing, branch, piece[:half], piece[half:].reshape(fsdp, small, width)


def shards(
    sizes,
    tokens,
    out_grad,
    slot_block,
    w_attend,
    w_mixing,
    w_expand,
    w_shrink,
    w_norms,
    first_attend,
    first_mixing,
    first_expand,
    first_shrink,
    first_norms,
    second_attend,
    second_mixing,
    second_expand,
    second_shrink,
    second_norms,
):
    fsdp, ctx = sizes
    f, c = lax.axis_index("fsdp"), lax.axis_index("ctx")
    rows, width = tokens.shape[1:]
    heads = width // HD // ctx
    lanes = heads * HD
    length = rows * ctx
    own = width // fsdp
    hidden = w_shrink.shape[0]

    place_of = slot_block[0]
    slot_of = jnp.sum(
        jnp.where(
            place_of[None, :] == jnp.arange(2 * ctx, dtype=jnp.int32)[:, None],
            jnp.arange(2 * ctx, dtype=jnp.int32)[None, :],
            0,
        ),
        axis=1,
    )

    start = tokens[0]
    incoming = out_grad[0]
    attend_grouped = (
        w_attend.reshape(own, 3, ctx, lanes).transpose(0, 2, 1, 3).reshape(own, 3 * width)
    )
    attend_here = lax.dynamic_slice_in_dim(
        w_attend.reshape(own, 3, width), c * lanes, lanes, 2
    ).reshape(own, 3 * lanes)
    padded_norms = jnp.concatenate([w_norms.astype(F32), jnp.zeros((4, own), F32)], axis=0)
    whole_tokens, whole_here, norms, expand_columns = start_exchange(
        start, attend_here, padded_norms, w_expand, hidden, sizes
    )
    norms = norms.transpose(1, 0, 2).reshape(8, width)
    whole_here = whole_here.reshape(width, 3 * lanes)
    whole_tokens, mixing_late, incoming_late, grouped_late = lax.optimization_barrier(
        (whole_tokens, w_mixing, incoming, attend_grouped)
    )
    whole_mixing = lax.all_gather(mixing_late, "fsdp", axis=0, tiled=True)
    grads_in = lax.all_gather(incoming_late, "fsdp", axis=0, tiled=True)
    whole_attend = lax.all_gather(grouped_late, "fsdp", axis=0, tiled=True)

    whole_tokens = whole_tokens.reshape(length, width)
    normed_all = (norm_parts(whole_tokens.astype(F32))[0] * norms[0] + norms[1]).astype(BF16)
    qkv = dot(normed_all, whole_here).astype(BF16)
    mixed_heads, out_t, total = attend_forward(slot_of, place_of, qkv, heads)
    mixed = ctx_to_rows(mixed_heads.reshape(ctx, rows, lanes), 1, sizes)

    middle = start.astype(F32) + dot(mixed, whole_mixing)
    normal_two, inverse_two = norm_parts(middle)
    normed_two = (normal_two * norms[2] + norms[3]).astype(BF16)
    normed_two_all = fsdp_gather(normed_two, 3, sizes).reshape(fsdp * rows, width)
    expanded = dot(normed_two_all, expand_columns)
    grad_activated = (
        lax.dot_general(
            grads_in, w_shrink, (((1,), (1,)), ((), ())), preferred_element_type=F32
        )
        .astype(BF16)
        .astype(F32)
    )
    activated, slope = gelu_and_slope(expanded)
    activated = activated.astype(BF16)
    grad_expanded = (grad_activated * slope).astype(BF16)
    part_normed_two = lax.dot_general(
        grad_expanded, expand_columns, (((1,), (1,)), ((), ())), preferred_element_type=F32
    ).astype(BF16)
    grad_normed_two = fsdp_scatter(part_normed_two.reshape(fsdp, rows, width), 4, sizes)
    part_out = dot(activated, w_shrink).astype(BF16)
    grad_shrink = lax.dot_general(
        activated, grads_in, (((0,), (0,)), ((), ())), preferred_element_type=F32
    ).astype(BF16)
    grad_expand = lax.dot_general(
        normed_two_all, grad_expanded, (((0,), (0,)), ((), ())), preferred_element_type=F32
    ).astype(BF16)
    grad_middle = incoming.astype(F32) + norm_back(
        grad_normed_two, norms[2], normal_two, inverse_two
    )
    grad_branch = grad_middle.astype(BF16)
    grad_mixed = lax.dot_general(
        grad_branch, whole_mixing, (((1,), (1,)), ((), ())), preferred_element_type=F32
    ).astype(BF16)
    grad_mixing = lax.dot_general(
        mixed, grad_branch, (((0,), (0,)), ((), ())), preferred_element_type=F32
    ).astype(BF16)
    grad_mixed, whole_attend = lax.optimization_barrier((grad_mixed, whole_attend))
    d_qkv, grad_joint, own_mixing, branch, shrink_piece, expand_piece = backward_exchange(
        slot_of, place_of, qkv, out_t, total, grad_mixed, grad_mixing, part_out,
        grad_shrink, grad_expand, heads, sizes,
    )
    layer_out = (middle + branch).astype(BF16)
    grad_normed = lax.dot_general(
        grad_joint, whole_attend, (((1,), (1,)), ((), ())), preferred_element_type=F32
    )
    normal_one, inverse_one = norm_parts(start.astype(F32))
    tokens_grad = (
        grad_middle + norm_back(grad_normed, norms[0], normal_one, inverse_one)
    )[None]
    zero = jnp.zeros((width,), F32)
    grad_norms = jnp.stack(
        [
            jnp.sum(grad_normed * normal_one, axis=0),
            jnp.sum(grad_normed, axis=0),
            jnp.sum(grad_normed_two * normal_two, axis=0),
            jnp.sum(grad_normed_two, axis=0),
        ]
        + [zero] * 4
    )
    part_attend = lax.dot_general(
        normed_all, d_qkv, (((0,), (0,)), ((), ())), preferred_element_type=F32
    ).astype(BF16)
    sum_attend, sum_mixing, parts_norms, sum_shrink, sum_expand = last_exchange(
        part_attend.reshape(fsdp, own, 3 * lanes),
        own_mixing,
        grad_norms.reshape(8, fsdp, own).transpose(1, 0, 2),
        shrink_piece,
        expand_piece,
        sizes,
    )
    sum_attend, sum_mixing = sum_attend.astype(F32), sum_mixing.astype(F32)
    sum_shrink, sum_expand = sum_shrink.astype(F32), sum_expand.astype(F32)
    sum_norms = jnp.sum(parts_norms, axis=0)[:4]

    result = [layer_out[None], tokens_grad]
    for weight, grad, first, second in (
        (w_attend, sum_attend, first_attend, second_attend),
        (w_mixing, sum_mixing, first_mixing, second_mixing),
        (w_expand, sum_expand, first_expand, second_expand),
        (w_shrink, sum_shrink, first_shrink, second_shrink),
        (w_norms, sum_norms, first_norms, second_norms),
    ):
        result.append(grad)
        result.extend(adam_step(weight, grad, first, second))
    return tuple(result)


def solution(mesh):
    rows = P("fsdp", None)
    columns = P(None, "fsdp")
    tokens = P("fsdp", "ctx", None)
    return jax.shard_map(
        functools.partial(shards, (mesh.shape["fsdp"], mesh.shape["ctx"])),
        mesh=mesh,
        in_specs=(tokens, tokens, rows)
        + (rows, rows, rows, rows, columns) * 3,
        out_specs=(tokens, tokens) + (rows,) * 16 + (columns,) * 4,
        check_vma=False,
    )
```

```python
import functools
import math

import jax
import jax.numpy as jnp
from jax import lax
from jax.experimental import pallas as pl
from jax.experimental.pallas import tpu as pltpu
from jax.sharding import PartitionSpec as P

HD = 64
STEP_COUNT = 10
EPS_NORM = 1e-05
NEG = -1e30
BETA_ONE = 0.9
BETA_TWO = 0.999
LEARN = 0.02
DECAY = 0.1
EPS_ADAM = 1e-08
CUBIC = 0.044715
ROOT_TWO_PI = math.sqrt(2.0 / math.pi)
LOG2E = math.log2(math.e)
TILE = 256
VMEM_LIMIT = 58 * 2**20
MESH = pl.DeviceIdType.MESH
F32 = jnp.float32
BF16 = jnp.bfloat16


def dot(left, right):
    return jnp.dot(left, right, preferred_element_type=F32)


def norm_parts(values):
    center = values - jnp.mean(values, axis=-1, keepdims=True)
    spread = jnp.mean(center * center, axis=-1, keepdims=True)
    inverse = lax.rsqrt(spread + EPS_NORM)
    return center * inverse, inverse


def norm_back(err, gain, normal, inverse):
    scaled = err * gain
    first = jnp.mean(scaled, axis=-1, keepdims=True)
    second = jnp.mean(scaled * normal, axis=-1, keepdims=True)
    return inverse * (scaled - first - normal * second)


def gelu_and_slope(values):
    square = values * values
    inner = ROOT_TWO_PI * values * (1.0 + CUBIC * square)
    tanh = jnp.tanh(inner)
    half = 0.5 * (1.0 + tanh)
    slope = half + 0.5 * values * (1.0 - tanh * tanh) * ROOT_TWO_PI * (
        1.0 + 3.0 * CUBIC * square
    )
    return values * half, slope


def adam_step(weight, grad, first, second):
    first_new = BETA_ONE * first + (1.0 - BETA_ONE) * grad
    second_new = BETA_TWO * second + (1.0 - BETA_TWO) * grad * grad
    mean_hat = first_new / (1.0 - BETA_ONE**STEP_COUNT)
    square_hat = second_new / (1.0 - BETA_TWO**STEP_COUNT)
    update = -LEARN * (
        mean_hat / (jnp.sqrt(square_hat) + EPS_ADAM) + DECAY * weight.astype(F32)
    )
    return (update, first_new, second_new)


def comm_call(kernel, out_shape, scratch, ident, operands, any_space=True):
    space = pl.ANY if any_space else pltpu.VMEM
    outs = jax.tree.map(lambda _: pl.BlockSpec(memory_space=space), out_shape)
    return pl.pallas_call(
        kernel,
        out_shape=out_shape,
        in_specs=[pl.BlockSpec(memory_space=space)] * len(operands),
        out_specs=outs,
        scratch_shapes=scratch,
        compiler_params=pltpu.CompilerParams(collective_id=ident, has_side_effects=True),
    )(*operands)


def remote(src, dst, send, recv, device):
    return pltpu.make_async_remote_copy(
        src_ref=src,
        dst_ref=dst,
        send_sem=send,
        recv_sem=recv,
        device_id=device,
        device_id_type=MESH,
    )


def fsdp_partners():
    f, c = lax.axis_index("fsdp"), lax.axis_index("ctx")
    x, k = f // 2, f % 2
    return f, c, x, k, x * 2 + 1 - k, (1 - x) * 2 + k


def greet(devices):
    barrier = pltpu.get_barrier_semaphore()
    for device in devices:
        pl.semaphore_signal(barrier, inc=1, device_id=device, device_id_type=MESH)
    pl.semaphore_wait(barrier, len(devices))


CHUNKS = 4


class Pieces:
    def __init__(self, send_sems, recv_sems):
        self.send_sems, self.recv_sems, self.used = send_sems, recv_sems, 0

    def copy(self, src, dst, device):
        n = self.used
        self.used += 1
        return remote(src, dst, self.send_sems.at[n], self.recv_sems.at[n], device)


def row_parts(rows, count):
    step = rows // count
    return [pl.ds(t * step, step) for t in range(count)]


class FsdpGather:
    def __init__(self, pieces, x_ref, o_ref, local_sem, chunks=CHUNKS):
        f, c, x, k, mate, across = fsdp_partners()
        self.parts = row_parts(x_ref.shape[0], chunks)
        self.local = pltpu.make_async_copy(x_ref, o_ref.at[f], local_sem)
        self.far = [
            pieces.copy(x_ref.at[p], o_ref.at[f, p], (across, c)) for p in self.parts
        ]
        self.near = pieces.copy(x_ref, o_ref.at[f], (mate, c))
        self.passed = [
            pieces.copy(o_ref.at[across, p], o_ref.at[across, p], (mate, c))
            for p in self.parts
        ]

    def start(self):
        for copy in self.far:
            copy.start()
        self.near.start()
        self.local.start()

    def forward(self):
        for copy, onward in zip(self.far, self.passed):
            copy.wait_recv()
            onward.start()

    def finish(self):
        self.local.wait()
        self.near.wait()
        for copy, onward in zip(self.far, self.passed):
            copy.wait_send()
            onward.wait()


class FsdpScatter:
    def __init__(self, pieces, x_ref, near_buf, far_out, far_in, chunks=CHUNKS):
        f, c, x, k, mate, across = fsdp_partners()
        self.parts = row_parts(x_ref.shape[1], chunks)
        self.x_ref, self.near_buf, self.far_out, self.far_in = x_ref, near_buf, far_out, far_in
        self.f, self.across = f, across
        away_mate = (1 - x) * 2 + 1 - k
        self.near_far = [
            pieces.copy(x_ref.at[away_mate, p], near_buf.at[0, p], (mate, c))
            for p in self.parts
        ]
        self.near_own = pieces.copy(x_ref.at[mate], near_buf.at[1], (mate, c))
        self.far = [pieces.copy(far_out.at[p], far_in.at[p], (across, c)) for p in self.parts]

    def start(self):
        for copy in self.near_far:
            copy.start()
        self.near_own.start()

    def forward(self):
        for p, near, far in zip(self.parts, self.near_far, self.far):
            near.wait_recv()
            self.far_out[p] = (
                self.x_ref[self.across, p].astype(F32) + self.near_buf[0, p].astype(F32)
            ).astype(BF16)
            far.start()

    def finish(self, store):
        self.near_own.wait_recv()
        for p, far in zip(self.parts, self.far):
            far.wait_recv()
            store(
                p,
                self.x_ref[self.f, p].astype(F32)
                + self.near_buf[1, p].astype(F32)
                + self.far_in[p].astype(F32),
            )
        self.near_own.wait_send()
        for near, far in zip(self.near_far, self.far):
            near.wait_send()
            far.wait_send()


class CtxGather:
    def __init__(self, x_ref, o_ref, local_sem, send_sem, recv_sem):
        f, c = lax.axis_index("fsdp"), lax.axis_index("ctx")
        self.f, self.c, self.z, self.y = f, c, c // 2, c % 2
        self.depth = o_ref.shape[0] // 2
        self.mate = self.z * 2 + 1 - self.y
        rows = x_ref.shape[0]
        some = rows * 7 // 16 // 8 * 8
        if some >= 32:
            self.parts = [pl.ds(0, some), pl.ds(some, some), pl.ds(2 * some, rows - 2 * some)]
            self.direct, self.turned = (0, 1), (2,)
        elif rows > 8:
            self.parts = [pl.ds(0, rows * 3 // 4), pl.ds(rows * 3 // 4, rows // 4)]
            self.direct, self.turned = (0,), (1,)
        else:
            self.parts = [pl.ds(0, rows)]
            self.direct, self.turned = (), (0,)
        self.x_ref, self.o_ref, self.send_sem, self.recv_sem = x_ref, o_ref, send_sem, recv_sem
        self.local = pltpu.make_async_copy(x_ref, o_ref.at[c], local_sem)

    @staticmethod
    def semaphores(n):
        return [
            pltpu.SemaphoreType.DMA,
            pltpu.SemaphoreType.DMA((n, 3, 3)),
            pltpu.SemaphoreType.DMA((n, 3)),
        ]

    def copy(self, zz, yy, part, way, own=False):
        block = zz * 2 + yy
        src = self.x_ref.at[self.parts[part]] if own else self.o_ref.at[block, self.parts[part]]
        there = (self.c - 2, self.c + 2, self.mate)[way]
        return remote(
            src,
            self.o_ref.at[block, self.parts[part]],
            self.send_sem.at[block, part, way],
            self.recv_sem.at[block, part],
            (self.f, there),
        )

    def both_ways(self, zz, yy, part, own=False):
        pl.when(self.z < self.depth - 1)(lambda: self.copy(zz, yy, part, 1, own).start())
        pl.when(self.z > 0)(lambda: self.copy(zz, yy, part, 0, own).start())

    def start(self):
        z, y = self.z, self.y
        for part in self.turned:
            self.copy(z, y, part, 2, True).start()
        for part in self.direct:
            self.both_ways(z, y, part, True)
            self.copy(z, y, part, 2, True).start()
        for part in self.turned:
            self.both_ways(z, y, part, True)
        self.local.start()

    def arrive(self, zz, yy, part, way):
        self.copy(zz, yy, part, way).wait_recv()
        if way == 1:
            pl.when(self.z < self.depth - 1)(lambda: self.copy(zz, yy, part, 1).start())
        else:
            pl.when(self.z > 0)(lambda: self.copy(zz, yy, part, 0).start())
        if part in self.direct:
            self.copy(zz, yy, part, 2).start()

    def along(self, step, yy, part):
        z = self.z
        pl.when(z - step >= 0)(lambda: self.arrive(z - step, yy, part, 1))
        pl.when(z + step < self.depth)(lambda: self.arrive(z + step, yy, part, 0))

    def step(self, step):
        z, y = self.z, self.y

        for part in self.direct:
            self.along(step, y, part)
        for part in self.turned:
            self.along(step, y, part)

            @pl.when(step == 1)
            def _():
                self.copy(z, 1 - y, part, 2).wait_recv()
                self.both_ways(z, 1 - y, part)

            self.along(step, 1 - y, part)

    def other(self, zz):
        for part in self.direct:
            self.copy(zz, 1 - self.y, part, 2).wait_recv()

    def others(self):
        z = self.z
        self.local.wait()
        self.other(z)
        for step in range(1, self.depth):
            pl.when(z - step >= 0)(lambda: self.other(z - step))
            pl.when(z + step < self.depth)(lambda: self.other(z + step))

    def sent(self):
        z, y, depth = self.z, self.y, self.depth
        blocks = [(y, part) for part in self.direct]
        for part in self.turned:
            blocks += [(y, part), (1 - y, part)]

        @pl.loop(0, depth)
        def _(step):
            for yy, part in blocks:

                def sent_right():
                    self.copy(z - step, yy, part, 1).wait_send()

                def sent_left():
                    self.copy(z + step, yy, part, 0).wait_send()

                pl.when((z - step >= 0) & (z < depth - 1))(sent_right)
                pl.when((z + step < depth) & (z > 0))(sent_left)

            for part in self.direct:
                pl.when((z - step >= 0) & (step > 0))(
                    lambda: self.copy(z - step, y, part, 2).wait_send()
                )
                pl.when(z + step < depth)(lambda: self.copy(z + step, y, part, 2).wait_send())

        for part in self.turned:
            self.copy(z, y, part, 2).wait_send()


def greet_lines(others, depth):
    f, c = lax.axis_index("fsdp"), lax.axis_index("ctx")
    z = c // 2
    barrier = pltpu.get_barrier_semaphore()

    def signal(device):
        pl.semaphore_signal(barrier, inc=1, device_id=device, device_id_type=MESH)

    for device in others:
        signal(device)
    pl.when(z > 0)(lambda: signal((f, c - 2)))
    pl.when(z < depth - 1)(lambda: signal((f, c + 2)))
    pl.semaphore_wait(
        barrier, len(others) + (z + depth - 1) // depth + (2 * depth - 2 - z) // depth
    )


def scatter_buffers(rows, width):
    return [
        pltpu.VMEM((2, rows, width), BF16),
        pltpu.VMEM((rows, width), BF16),
        pltpu.VMEM((rows, width), BF16),
    ]


class CtxExchange:
    def __init__(self, pieces, n, source, target, local_sems):
        f, c = lax.axis_index("fsdp"), lax.axis_index("ctx")
        self.copies = []
        for j in range(n - 1, 0, -1):
            there = (c + j) % n
            for src, dst in zip(source(there), target(c)):
                self.copies.append(pieces.copy(src, dst, (f, there)))
        self.local = [
            pltpu.make_async_copy(src, dst, sem)
            for src, dst, sem in zip(source(c), target(c), local_sems)
        ]

    def start(self):
        for copy in self.copies + self.local:
            copy.start()

    def finish(self):
        for copy in self.local + self.copies:
            copy.wait()


def greet_ctx(n, others=()):
    f, c = lax.axis_index("fsdp"), lax.axis_index("ctx")
    greet([(f, (c + j) % n) for j in range(1, n)] + list(others))


def column_block(ref, block, lanes):
    return ref.at[:, pl.ds(pl.multiple_of(block * lanes, 128), lanes)]


def ctx_to_rows(values):
    n, rows, lanes = values.shape
    moved = lax.all_to_all(values, "ctx", split_axis=0, concat_axis=0, tiled=True)
    return moved.transpose(1, 0, 2).reshape(rows, n * lanes)


def ctx_to_heads(values, n):
    rows, lanes = values.shape[0], values.shape[1] // n
    return lax.all_to_all(
        values.reshape(rows, n, lanes).transpose(1, 0, 2),
        "ctx",
        split_axis=0,
        concat_axis=0,
        tiled=True,
    )


def last_kernel(
    n, attend_ref, mixing_ref, sums_ref, shrink_ref, expand_ref, joint_ref, weight_ref,
    start_ref, gains_ref,
    attend_out, mixing_out, norms_out, shrink_out, expand_out, back_ref,
    mixing_in, norms_part, norms_in, norms_own, block, blocks, expand_own,
    joint, weight, err,
    send_sems, recv_sems, local_sems, *gather_sems,
):
    f, c, x, k, mate, across = fsdp_partners()
    lanes = mixing_in.shape[-1]
    own, wide = attend_ref.shape
    hidden = expand_ref.shape[-1]
    width = err.shape[1]
    others = [(f + j) % 4 for j in (1, 2, 3)]
    loads = [
        pltpu.make_async_copy(joint_ref, joint, local_sems.at[0]),
        pltpu.make_async_copy(weight_ref, weight, local_sems.at[1]),
    ]
    for copy in loads:
        copy.start()
    greet_ctx(n, [(o, c) for o in others])
    pieces = Pieces(send_sems, recv_sems)
    sems = [gather_sems[3 * j : 3 * j + 3] for j in range(4)]

    def columns(j):
        return expand_own.at[:, pl.ds(pl.multiple_of(j * hidden, 128), hidden)]

    early = [pieces.copy(expand_ref.at[o], columns(f), (o, c)) for o in others]
    early += [pltpu.make_async_copy(expand_ref.at[f], columns(f), local_sems.at[2])]
    move = CtxExchange(
        pieces,
        n,
        lambda j: [column_block(mixing_ref, j, lanes)],
        lambda j: [mixing_in.at[j]],
        [local_sems.at[3]],
    )
    for copy in early:
        copy.start()
    move.start()
    shrink = CtxGather(shrink_ref, shrink_out, *sems[0])
    expand = CtxGather(expand_own, expand_out, *sems[1])
    small = CtxGather(norms_own, norms_out, *sems[2])
    gather = CtxGather(block, blocks, *sems[3])
    shrink.start()
    for copy in early:
        copy.wait()
    expand.start()
    for copy in loads:
        copy.wait()
    shrink.step(1)

    def multiply(first, last):
        @pl.loop(first, last)
        def _(j):
            cols = pl.ds(pl.multiple_of(j * TILE, TILE), TILE)
            err[:, cols] = dot_last(joint[...], weight[cols, :])

    multiply(0, width // TILE // 2)
    expand.step(1)
    move.finish()
    total = mixing_in[0].astype(F32)
    for j in range(1, n):
        total += mixing_in[j].astype(F32)
    block[:, wide:] = total.astype(BF16)
    block[:, :wide] = attend_ref[...]
    gather.start()
    shrink.step(2)
    multiply(width // TILE // 2, width // TILE)
    expand.step(2)
    sums = [jnp.zeros((1, width), F32)] * 2
    for t in range(err.shape[0] // 64):
        part = slice(t * 64, (t + 1) * 64)
        one, scale = norm_parts(start_ref[part].astype(F32))
        value = err[part]
        sums[0] += jnp.sum(value * one, axis=0, keepdims=True)
        sums[1] += jnp.sum(value, axis=0, keepdims=True)
        back_ref[part] = norm_back(value, gains_ref[0:1, :], one, scale)
    for j in range(4):
        cols = slice(j * own, (j + 1) * own)
        norms_part[j] = sums_ref[:, cols]
        norms_part[j, 0:1] = sums[0][:, cols]
        norms_part[j, 1:2] = sums[1][:, cols]
    late = [pieces.copy(norms_part.at[o], norms_in.at[f], (o, c)) for o in others]
    for copy in late:
        copy.start()
    norms_in[f] = norms_part[f]
    gather.step(1)
    for copy in late:
        copy.wait()
    norms_own[...] = norms_in[0] + norms_in[1] + norms_in[2] + norms_in[3]
    small.start()
    shrink.step(3)
    expand.step(3)
    small.step(1)
    gather.step(2)
    small.step(2)
    gather.step(3)
    small.step(3)
    for each in (gather, small, shrink, expand):
        each.others()
    for j in range(n):
        for part in range(3):
            at = (part * n + j) * lanes
            attend_out[:, at : at + lanes] = blocks[j, :, part * lanes : (part + 1) * lanes]
        mixing_out[:, j * lanes : (j + 1) * lanes] = blocks[j, :, wide:]
    for each in (shrink, expand, small, gather):
        each.sent()


def last_exchange(
    own_attend, own_mixing, norm_sums, shrink_piece, expand_piece, joint, whole_attend, start,
    norms, sizes,
):
    fsdp, n = sizes
    own, wide = own_attend.shape
    rows, width = start.shape
    lanes = width // n
    _, piece, hidden = expand_piece.shape
    if sizes != (4, 8):
        attend = (
            lax.all_gather(own_attend, "ctx", axis=0, tiled=False)
            .reshape(n, own, 3, lanes)
            .transpose(1, 2, 0, 3)
            .reshape(own, 3 * width)
        )
        err = dot_last(joint, whole_attend)
        one, scale = norm_parts(start.astype(F32))
        sums = jnp.concatenate(
            [jnp.sum(err * one, axis=0)[None], jnp.sum(err, axis=0)[None], norm_sums[2:]], axis=0
        )
        parts = lax.psum_scatter(
            sums.reshape(8, fsdp, own).transpose(1, 0, 2),
            "fsdp",
            scatter_dimension=0,
            tiled=False,
        )
        expand = lax.all_to_all(expand_piece, "fsdp", split_axis=0, concat_axis=0, tiled=True)
        expand = expand.transpose(1, 0, 2).reshape(piece, fsdp * hidden)
        return (
            attend,
            lax.psum(own_mixing, "ctx"),
            lax.all_gather(parts, "ctx", axis=0, tiled=False),
            lax.all_gather(shrink_piece, "ctx", axis=0, tiled=True),
            lax.all_gather(expand, "ctx", axis=0, tiled=True),
            norm_back(err, norms[0], one, scale),
        )
    count = n - 1 + 6
    vmem, anywhere = pl.BlockSpec(memory_space=pltpu.VMEM), pl.BlockSpec(memory_space=pl.ANY)
    attend, mixing, parts, shrink, expand, back = pl.pallas_call(
        functools.partial(last_kernel, n),
        out_shape=(
            jax.ShapeDtypeStruct((own, 3 * width), BF16),
            jax.ShapeDtypeStruct((own, width), BF16),
            jax.ShapeDtypeStruct((n, 8, own), F32),
            jax.ShapeDtypeStruct((n,) + shrink_piece.shape, BF16),
            jax.ShapeDtypeStruct((n, piece, fsdp * hidden), BF16),
            jax.ShapeDtypeStruct((rows, width), F32),
        ),
        in_specs=[vmem, vmem, vmem] + [anywhere] * 4 + [vmem] * 2,
        out_specs=(vmem, vmem, vmem, anywhere, anywhere, vmem),
        scratch_shapes=[
            pltpu.VMEM((n, own, lanes), BF16),
            pltpu.VMEM((fsdp, 8, own), F32),
            pltpu.VMEM((fsdp, 8, own), F32),
            pltpu.VMEM((8, own), F32),
            pltpu.VMEM((own, wide + lanes), BF16),
            pltpu.VMEM((n, own, wide + lanes), BF16),
            pltpu.VMEM((piece, fsdp * hidden), BF16),
            pltpu.VMEM((rows, 3 * width), BF16),
            pltpu.VMEM((width, 3 * width), BF16),
            pltpu.VMEM((rows, width), F32),
            pltpu.SemaphoreType.DMA((count,)),
            pltpu.SemaphoreType.DMA((count,)),
            pltpu.SemaphoreType.DMA((4,)),
        ]
        + CtxGather.semaphores(n) * 4,
        compiler_params=pltpu.CompilerParams(
            collective_id=7, has_side_effects=True, vmem_limit_bytes=VMEM_LIMIT
        ),
    )(
        own_attend, own_mixing, norm_sums, shrink_piece, expand_piece, joint, whole_attend,
        start, norms,
    )
    return (
        attend,
        mixing,
        parts,
        shrink.reshape(n * shrink_piece.shape[0], width),
        expand.reshape(n * piece, fsdp * hidden),
        back,
    )


def head_rows(h):
    return slice(h * HD, (h + 1) * HD)


def attend_forward_kernel(
    heads, slot_ref, place_ref, qkv_ref, mixed_ref, out_t_ref, total_ref,
    q_pos, k_pos, v_pos, q_t, v_t, scores, o_pos,
):
    length, lanes = q_pos.shape
    blocks = slot_ref.shape[0]
    size = length // blocks
    tiles = length // TILE
    factor = LOG2E / math.sqrt(HD)
    for p in range(blocks):
        rows = qkv_ref[pl.ds(slot_ref[p] * size, size), :]
        here = slice(p * size, (p + 1) * size)
        q_pos[here, :] = rows[:, :lanes]
        k_pos[here, :] = rows[:, lanes : 2 * lanes]
        v_pos[here, :] = rows[:, 2 * lanes :]
    for t in range(tiles):
        here = slice(t * TILE, (t + 1) * TILE)
        q_t[:, here] = q_pos[here, :].T
        v_t[:, here] = v_pos[here, :].T
    head_of_row = lax.broadcasted_iota(jnp.int32, (lanes, TILE), 0) // HD
    allowed = lax.broadcasted_iota(jnp.int32, (TILE, TILE), 0) <= lax.broadcasted_iota(
        jnp.int32, (TILE, TILE), 1
    )

    def fold_max(values):
        return jnp.max(values.reshape(TILE // 8, 8, TILE), axis=0)

    def fold_sum(values):
        return jnp.sum(values.reshape(TILE // 8, 8, TILE), axis=0)

    @pl.loop(0, tiles)
    def _(i):
        here = pl.ds(pl.multiple_of(i * TILE, TILE), TILE)
        q_tile = q_t[:, here]
        q_heads = [
            jnp.where(head_of_row == h, q_tile, jnp.zeros_like(q_tile)) for h in range(heads)
        ]

        def first(j, tops):
            there = pl.ds(pl.multiple_of(j * TILE, TILE), TILE)
            keys = k_pos[there, :]
            result = []
            for h in range(heads):
                raw = dot(keys, q_heads[h])
                scores[h, there, :] = raw
                result.append(jnp.maximum(tops[h], fold_max(raw)))
            return tuple(result)

        tops = lax.fori_loop(
            0, i, first, tuple(jnp.full((8, TILE), NEG, F32) for _ in range(heads))
        )
        keys = k_pos[here, :]
        row_tops = []
        for h in range(heads):
            raw = jnp.where(allowed, dot(keys, q_heads[h]), NEG)
            scores[h, here, :] = raw
            row_tops.append(
                jnp.max(jnp.maximum(tops[h], fold_max(raw)), axis=0, keepdims=True) * factor
            )

        def second(j, state):
            there = pl.ds(pl.multiple_of(j * TILE, TILE), TILE)
            result = []
            for h in range(heads):
                sums, acc = state[h]
                probs = jnp.exp2(scores[h, there, :] * factor - row_tops[h])
                acc = acc + dot(v_t[head_rows(h), there], probs.astype(BF16))
                result.append((sums + fold_sum(probs), acc))
            return tuple(result)

        state = lax.fori_loop(
            0,
            i + 1,
            second,
            tuple(
                (jnp.zeros((8, TILE), F32), jnp.zeros((HD, TILE), F32)) for _ in range(heads)
            ),
        )
        outs = []
        for h in range(heads):
            sums, acc = state[h]
            row_sum = jnp.sum(sums, axis=0, keepdims=True)
            out = acc * (1.0 / row_sum)
            out_t_ref[head_rows(h), here] = out
            total_ref[pl.ds(h, 1), here] = row_tops[h] + jnp.log2(row_sum)
            outs.append(out)
        out = jnp.concatenate(outs, axis=0) if heads > 1 else outs[0]
        o_pos[here, :] = out.T.astype(BF16)

    for s in range(blocks):
        mixed_ref[s * size : (s + 1) * size, :] = o_pos[
            pl.ds(place_ref[s] * size, size), :
        ]


def attend_forward_scratch(length, heads):
    lanes = heads * HD
    return (
        [pltpu.VMEM((length, lanes), BF16)] * 3
        + [pltpu.VMEM((lanes, length), BF16)] * 2
        + [pltpu.VMEM((heads, length, TILE), F32), pltpu.VMEM((length, lanes), BF16)]
    )


def attend_forward(slot_of, place_of, qkv, heads):
    length = qkv.shape[0]
    lanes = heads * HD
    vmem = pl.BlockSpec(memory_space=pltpu.VMEM)
    smem = pl.BlockSpec(memory_space=pltpu.SMEM)
    return pl.pallas_call(
        functools.partial(attend_forward_kernel, heads),
        out_shape=(
            jax.ShapeDtypeStruct((length, lanes), BF16),
            jax.ShapeDtypeStruct((lanes, length), F32),
            jax.ShapeDtypeStruct((8, length), F32),
        ),
        in_specs=[smem, smem, vmem],
        out_specs=(vmem, vmem, vmem),
        scratch_shapes=attend_forward_scratch(length, heads),
        cost_estimate=pl.CostEstimate(
            flops=4 * length * length * lanes,
            bytes_accessed=10 * length * lanes,
            transcendentals=heads * length * length // 2,
        ),
    )(slot_of, place_of, qkv)


def forward_kernel(
    heads, slot_ref, place_ref, tokens_ref, attend_ref, norms_ref, expand_ref, mixing_ref, grad_ref,
    mixed_ref, out_t_ref, total_ref, qkv_ref, norms_out, normed_out, expand_out, mixing_out, grad_out,
    q_pos, k_pos, v_pos, q_t, v_t, scores, o_pos,
    tokens, attend_own, attend, normed, pick_sems, store_sem, local_sems, send_sems, recv_sems, ctx_local, ctx_send, ctx_recv,
):
    f, c, x, k, mate, across = fsdp_partners()
    n, rows, width = tokens.shape
    depth = n // 2
    z, y = c // 2, c % 2
    others = [(f + j) % 4 for j in (1, 2, 3)]
    greet_lines([(o, c) for o in others] + [(f, z * 2 + 1 - y)], depth)
    pieces = Pieces(send_sems, recv_sems)
    gather = CtxGather(tokens_ref, tokens, ctx_local, ctx_send, ctx_recv)
    gather.start()
    weights = FsdpGather(pieces, attend_own, attend, local_sems.at[0], 2)
    lanes = heads * HD
    picks = [
        pltpu.make_async_copy(
            column_block(attend_ref, part * n + c, lanes),
            attend_own.at[:, part * lanes : (part + 1) * lanes],
            pick_sems.at[part],
        )
        for part in range(3)
    ]
    for copy in picks:
        copy.start()
    for copy in picks:
        copy.wait()
    mixing = FsdpGather(pieces, mixing_ref, mixing_out, local_sems.at[1], 2)
    grads = FsdpGather(pieces, grad_ref, grad_out, local_sems.at[2], 2)
    weights.start()
    own, hidden = expand_ref.shape[0], expand_out.shape[1]
    norms = [pieces.copy(norms_ref, norms_out.at[f], (o, c)) for o in others]

    def columns(o):
        return (
            expand_ref.at[:, pl.ds(pl.multiple_of(o * hidden, 128), hidden)],
            expand_out.at[pl.ds(pl.multiple_of(f * own, 16), own)],
        )

    expands = [pieces.copy(*columns(o), (o, c)) for o in others]
    expands.append(pltpu.make_async_copy(*columns(f), local_sems.at[3]))
    for copy in norms + expands:
        copy.start()
    mixing.start()
    grads.start()
    norms_out[f] = norms_ref[...]
    for copy in norms:
        copy.wait()
    weights.forward()
    weights.finish()

    def process(block):
        @pl.loop(0, rows // 64)
        def _(t):
            part = pl.ds(pl.multiple_of(t * 64, 64), 64)
            value = norm_parts(tokens[block, part].astype(F32))[0]
            for j in range(4):
                cols = slice(j * own, (j + 1) * own)
                normed[block, part, cols] = (
                    value[:, cols] * norms_out[j, 0:1] + norms_out[j, 1:2]
                ).astype(BF16)

        at = pl.ds(pl.multiple_of(block * rows, 128), rows)
        qkv_ref[at] = dot(normed[block], attend[...].reshape(width, attend.shape[-1])).astype(BF16)

    @pl.loop(0, depth + 1)
    def _(step):
        @pl.when((step > 0) & (step < depth))
        def _():
            gather.step(step)

        @pl.loop(0, 4)
        def _(q):
            turn, down = q // 2, q % 2
            far = step - turn
            zz = z + (1 - 2 * down) * far
            yy = y * (1 - turn) + (1 - y) * turn
            valid = (far >= 0) & (far < depth) & (zz >= 0) & (zz < depth) & (far + 1 - down > 0)

            @pl.when(valid)
            def _():
                @pl.when(step == 0)
                def _():
                    gather.local.wait()

                @pl.when(turn == 1)
                def _():
                    gather.other(zz)

                process(zz * 2 + yy)

    store = pltpu.make_async_copy(normed, normed_out, store_sem)
    store.start()
    attend_forward_kernel(
        heads, slot_ref, place_ref, qkv_ref, mixed_ref, out_t_ref, total_ref,
        q_pos, k_pos, v_pos, q_t, v_t, scores, o_pos,
    )
    mixing.forward()
    grads.forward()
    mixing.finish()
    grads.finish()
    for copy in expands:
        copy.wait()
    gather.sent()
    store.wait()


def forward_stage(
    slot_of, place_of, tokens, w_attend, norms, w_expand, w_mixing, incoming, hidden, heads, sizes
):
    fsdp, n = sizes
    rows, width = tokens.shape
    length, lanes = n * rows, heads * HD
    own = w_mixing.shape[0]
    if sizes != (4, 8):
        columns = lax.all_to_all(
            w_expand.reshape(own, fsdp, hidden).transpose(1, 0, 2),
            "fsdp",
            split_axis=0,
            concat_axis=0,
            tiled=True,
        ).reshape(fsdp * own, hidden)
        everything = lax.all_gather(tokens, "ctx", axis=0, tiled=True)
        attend_here = lax.dynamic_slice_in_dim(
            w_attend.reshape(own, 3, width), lax.axis_index("ctx") * lanes, lanes, 2
        ).reshape(own, 3 * lanes)
        weights = lax.all_gather(attend_here, "fsdp", axis=0, tiled=True)
        gains = lax.all_gather(norms, "fsdp", axis=1, tiled=True)
        normed = (norm_parts(everything.astype(F32))[0] * gains[0] + gains[1]).astype(BF16)
        qkv = dot(normed, weights).astype(BF16)
        mixed, out_t, total = attend_forward(slot_of, place_of, qkv, heads)
        return (
            mixed,
            out_t,
            total,
            qkv,
            gains,
            normed,
            columns,
            lax.all_gather(w_mixing, "fsdp", axis=0, tiled=True),
            lax.all_gather(incoming, "fsdp", axis=0, tiled=True),
        )
    vmem, anywhere = pl.BlockSpec(memory_space=pltpu.VMEM), pl.BlockSpec(memory_space=pl.ANY)
    smem = pl.BlockSpec(memory_space=pltpu.SMEM)
    count = 3 * (2 * 2 + 1) + 6
    mixed, out_t, total, qkv, gains, normed, columns, mixing, grads = pl.pallas_call(
        functools.partial(forward_kernel, heads),
        out_shape=(
            jax.ShapeDtypeStruct((length, lanes), BF16),
            jax.ShapeDtypeStruct((lanes, length), F32),
            jax.ShapeDtypeStruct((8, length), F32),
            jax.ShapeDtypeStruct((length, 3 * lanes), BF16),
            jax.ShapeDtypeStruct((fsdp, 8, own), F32),
            jax.ShapeDtypeStruct((n, rows, width), BF16),
            jax.ShapeDtypeStruct((fsdp * own, hidden), BF16),
            jax.ShapeDtypeStruct((fsdp, own, width), BF16),
            jax.ShapeDtypeStruct((fsdp, rows, width), BF16),
        ),
        in_specs=[smem, smem, anywhere, anywhere, vmem] + [anywhere] * 3,
        out_specs=(vmem,) * 5 + (anywhere,) * 4,
        scratch_shapes=attend_forward_scratch(length, heads)
        + [
            pltpu.VMEM((n, rows, width), BF16),
            pltpu.VMEM((own, 3 * lanes), BF16),
            pltpu.VMEM((fsdp, own, 3 * lanes), BF16),
            pltpu.VMEM((n, rows, width), BF16),
            pltpu.SemaphoreType.DMA((3,)),
            pltpu.SemaphoreType.DMA,
            pltpu.SemaphoreType.DMA((4,)),
            pltpu.SemaphoreType.DMA((count,)),
            pltpu.SemaphoreType.DMA((count,)),
        ]
        + CtxGather.semaphores(n),
        compiler_params=pltpu.CompilerParams(
            collective_id=0, has_side_effects=True, vmem_limit_bytes=VMEM_LIMIT
        ),
    )(slot_of, place_of, tokens, w_attend, norms, w_expand, w_mixing, incoming)
    return (
        mixed,
        out_t,
        total,
        qkv,
        gains.transpose(1, 0, 2).reshape(8, width),
        normed.reshape(length, width),
        columns,
        mixing.reshape(width, width),
        grads.reshape(fsdp * rows, width),
    )


def attend_backward_kernel(
    heads, between, slot_ref, place_ref, qkv_ref, load_grad, out_t_ref, total_ref, result_ref,
    q_pos, k_pos, v_pos, g_pos, k_heads, v_heads, q_t, k_t, g_t, delta,
    dq_t, dk_acc, dv_acc, d_pos,
):
    length, lanes = q_pos.shape
    blocks = slot_ref.shape[0]
    size = length // blocks
    tiles = length // TILE
    scale = 1.0 / math.sqrt(HD)
    factor = LOG2E * scale
    for p in range(blocks):
        rows = qkv_ref[pl.ds(slot_ref[p] * size, size), :]
        here = slice(p * size, (p + 1) * size)
        q_pos[here, :] = rows[:, :lanes]
        k_pos[here, :] = rows[:, lanes : 2 * lanes]
        v_pos[here, :] = rows[:, 2 * lanes :]
    head_of_lane = lax.broadcasted_iota(jnp.int32, (TILE, lanes), 1) // HD
    allowed = lax.broadcasted_iota(jnp.int32, (TILE, TILE), 0) <= lax.broadcasted_iota(
        jnp.int32, (TILE, TILE), 1
    )
    for t in range(tiles):
        here = slice(t * TILE, (t + 1) * TILE)
        q_t[:, here] = q_pos[here, :].T
        k_t[:, here] = k_pos[here, :].T
        keys, values = k_pos[here, :], v_pos[here, :]
        for h in range(heads):
            k_heads[h, here, :] = jnp.where(head_of_lane == h, keys, jnp.zeros_like(keys))
            v_heads[h, here, :] = jnp.where(head_of_lane == h, values, jnp.zeros_like(values))
    dq_t[...] = jnp.zeros_like(dq_t)
    load = load_grad()
    for p in range(blocks):
        g_pos[p * size : (p + 1) * size, :] = load(slot_ref[p] * size, size)
    for t in range(tiles):
        here = slice(t * TILE, (t + 1) * TILE)
        g_tile = g_pos[here, :].T
        g_t[:, here] = g_tile
        product = g_tile.astype(F32) * out_t_ref[:, here]
        for h in range(heads):
            delta[h : h + 1, here] = jnp.sum(product[head_rows(h)], axis=0, keepdims=True)

    def pair(j, i, masked):
        there = pl.ds(pl.multiple_of(j * TILE, TILE), TILE)
        here = pl.ds(pl.multiple_of(i * TILE, TILE), TILE)
        for h in range(heads):
            raw = dot(k_heads[h, there, :], q_t[:, here])
            probs = jnp.exp2(raw * factor - total_ref[pl.ds(h, 1), here])
            if masked:
                probs = jnp.where(allowed, probs, 0.0)
            d_probs = dot(v_heads[h, there, :], g_t[:, here])
            d_scores = (probs * (d_probs - delta[pl.ds(h, 1), here])).astype(BF16)
            dv = dot(probs.astype(BF16), g_pos[here, :])
            dk = dot(d_scores, q_pos[here, :])
            if masked:
                dv_acc[h], dk_acc[h] = dv, dk
            else:
                dv_acc[h] += dv
                dk_acc[h] += dk
            dq_t[head_rows(h), here] += dot(k_t[head_rows(h), there], d_scores)

    @pl.loop(0, tiles)
    def _(j):
        pair(j, j, True)

        @pl.loop(j + 1, tiles)
        def _(i):
            pair(j, i, False)

        there = pl.ds(pl.multiple_of(j * TILE, TILE), TILE)
        for index, acc, weight in ((1, dk_acc, scale), (2, dv_acc, 1.0)):
            value = acc[0]
            for h in range(1, heads):
                value = jnp.where(head_of_lane == h, acc[h], value)
            d_pos[there, index * lanes : (index + 1) * lanes] = (value * weight).astype(BF16)
        between(j)

    for t in range(tiles):
        here = slice(t * TILE, (t + 1) * TILE)
        d_pos[here, :lanes] = (dq_t[:, here].T * scale).astype(BF16)
    for s in range(blocks):
        result_ref[s * size : (s + 1) * size, :] = d_pos[pl.ds(place_ref[s] * size, size), :]


def attend_backward_scratch(length, heads):
    lanes = heads * HD
    rows = pltpu.VMEM((length, lanes), BF16)
    columns = pltpu.VMEM((lanes, length), BF16)
    by_head = pltpu.VMEM((heads, length, lanes), BF16)
    return (
        [rows] * 4
        + [by_head] * 2
        + [columns] * 3
        + [
            pltpu.VMEM((8, length), F32),
            pltpu.VMEM((lanes, length), F32),
            pltpu.VMEM((heads, TILE, lanes), F32),
            pltpu.VMEM((heads, TILE, lanes), F32),
            pltpu.VMEM((length, 3 * lanes), BF16),
        ]
    )


ATTEND_SCRATCH = 14


def local_backward_kernel(
    heads, slot_ref, place_ref, qkv_ref, grad_ref, out_t_ref, total_ref, result_ref, *scratch
):
    attend_backward_kernel(
        heads, lambda j: None, slot_ref, place_ref, qkv_ref,
        lambda: lambda at, size: grad_ref[pl.ds(at, size), :],
        out_t_ref, total_ref, result_ref, *scratch,
    )


def attend_backward(slot_of, place_of, qkv, grad, out_t, total, heads):
    length = qkv.shape[0]
    lanes = heads * HD
    vmem = pl.BlockSpec(memory_space=pltpu.VMEM)
    smem = pl.BlockSpec(memory_space=pltpu.SMEM)
    return pl.pallas_call(
        functools.partial(local_backward_kernel, heads),
        out_shape=jax.ShapeDtypeStruct((length, 3 * lanes), BF16),
        in_specs=[smem, smem, vmem, vmem, vmem, vmem],
        out_specs=vmem,
        scratch_shapes=attend_backward_scratch(length, heads),
    )(slot_of, place_of, qkv, grad, out_t, total)


def backward_kernel(
    n, heads, slot_ref, place_ref, qkv_ref, out_t_ref, total_ref,
    mixed_ref, mixing_ref, out_ref, shrink_ref, expand_ref, normed_ref, weight_ref,
    joint_ref, own_mixing_ref, branch_ref, piece_ref, own_attend_ref, whole_ref, *rest,
):
    scratch, rest = rest[:ATTEND_SCRATCH], rest[ATTEND_SCRATCH:]
    (
        result, grad_in, normed, part_attend,
        near_a, far_out_a, far_in_a, near_b, far_out_b, far_in_b, near_c, far_out_c, far_in_c,
        pair_in, pair_sum, line_in, load_sem, local_sems, send_sems, recv_sems,
        pair_send, pair_recv, line_send, line_recv,
    ) = rest
    f, c, x, k, mate, across = fsdp_partners()
    depth = n // 2
    z, y = c // 2, c % 2
    lanes = heads * HD
    half = shrink_ref.shape[1]
    fsdp, _, small, hidden = expand_ref.shape
    length, width = normed.shape
    rows = length // n
    own = width // fsdp
    load = pltpu.make_async_copy(normed_ref, normed, load_sem)
    load.start()
    greet_ctx(n, [(mate, c), (across, c)])
    pieces = Pieces(send_sems, recv_sems)
    to_heads = CtxExchange(
        pieces, n, lambda j: [column_block(mixed_ref, j, lanes)], lambda j: [grad_in.at[j]],
        [local_sems.at[0]],
    )
    to_rows = CtxExchange(
        pieces,
        n,
        lambda j: [
            result.at[pl.ds(pl.multiple_of(j * rows, 128), rows), part * lanes : (part + 1) * lanes]
            for part in range(3)
        ],
        lambda j: [column_block(joint_ref, part * n + j, lanes) for part in range(3)],
        [local_sems.at[1 + part] for part in range(3)],
    )
    mixing = FsdpScatter(pieces, mixing_ref, near_a, far_out_a, far_in_a)
    branch = FsdpScatter(pieces, out_ref, near_b, far_out_b, far_in_b)
    attend = FsdpScatter(pieces, part_attend, near_c, far_out_c, far_in_c, 2)
    weights = FsdpGather(pieces, weight_ref, whole_ref, local_sems.at[4])
    to_heads.start()

    side = z // 2
    inner = z * (1 - side) + (depth - 1 - z) * side

    def owner(t):
        place = depth - 1 - t + inner * (t // 2) * (2 * (t % 2) - 1)
        return place * (1 - 2 * side) + (depth - 1) * side

    def pair_copies(t):
        to = owner(t) * 2 + 1 - y
        there = (f, z * 2 + 1 - y)
        return [
            remote(
                shrink_ref.at[to], pair_in.at[t, pl.ds(0, half)],
                pair_send.at[t, 0], pair_recv.at[t, 0], there,
            )
        ] + [
            remote(
                expand_ref.at[j, to], pair_in.at[t, pl.ds(half + j * small, small)],
                pair_send.at[t, 1 + j], pair_recv.at[t, 1 + j], there,
            )
            for j in range(fsdp)
        ]

    def pair_wait(t):
        for copy in pair_copies(t):
            copy.wait_recv()

    def pair_total(t, store):
        to = owner(t) * 2 + y

        @pl.loop(0, half // small)
        def _(j):
            at = pl.ds(pl.multiple_of(j * small, small), small)
            store(at, shrink_ref[to, at].astype(F32) + pair_in[t, at].astype(F32))

        @pl.loop(0, fsdp)
        def _(j):
            at = pl.ds(pl.multiple_of(half + j * small, small), small)
            store(at, expand_ref[j, to].astype(F32) + pair_in[t, at].astype(F32))

    def line_copy(t):
        zz = owner(t)
        up = (zz + depth - z) // depth
        last = (1 - up) * ((depth - 1 - (z - 1 - zz)) // (depth - 1))
        slot = zz + (depth - zz) * last
        return remote(
            pair_sum.at[t], line_in.at[slot], line_send.at[t], line_recv.at[slot],
            (f, c + 4 * up - 2),
        )

    def line_wait(slot):
        remote(
            pair_sum.at[0], line_in.at[slot], line_send.at[0], line_recv.at[slot],
            (f, z * 2 + 1 - y),
        ).wait_recv()

    def pass_on(t):
        pair_wait(t)
        zz = owner(t)

        @pl.when(inner == 0)
        def _():
            def store(at, value):
                pair_sum[t, at] = value.astype(BF16)

            pair_total(t, store)

        @pl.when(inner > 0)
        def _():
            line_wait(zz)

            def store(at, value):
                pair_sum[t, at] = (value + line_in[zz, at].astype(F32)).astype(BF16)

            pair_total(t, store)

        line_copy(t).start()

    for t in range(depth):
        for copy in pair_copies(t):
            copy.start()
    mixing.start()
    branch.start()
    mixing.forward()
    branch.forward()
    weights.start()

    def load_grad():
        to_heads.finish()

        def load_rows(at, size):
            return grad_in[at // rows, pl.ds(at % rows, size), :]

        return load_rows

    def between(j):
        @pl.when(((j == 0) & (inner == 0)) | (j == 3))
        def _():
            pass_on(j // 3 * (1 - inner))

    attend_backward_kernel(
        heads, between, slot_ref, place_ref, qkv_ref, load_grad, out_t_ref, total_ref,
        result, *scratch,
    )
    to_rows.start()
    pass_on(2 - inner)
    pl.when(inner > 0)(lambda: pass_on(2))
    load.wait()

    @pl.loop(0, fsdp)
    def _(j):
        cols = pl.ds(pl.multiple_of(j * own, own), own)
        part_attend[j] = dot_first(normed[:, cols], result[...]).astype(BF16)

    attend.start()
    attend.forward()

    def store_mixing(p, value):
        own_mixing_ref[p] = value.astype(BF16)

    def store_branch(p, value):
        branch_ref[p] = value

    def store_attend(p, value):
        own_attend_ref[p] = value.astype(BF16)

    mixing.finish(store_mixing)
    branch.finish(store_branch)
    weights.forward()
    attend.finish(store_attend)
    pair_wait(depth - 1)
    pl.when(z > 0)(lambda: line_wait(z))
    pl.when(z < depth - 1)(lambda: line_wait(depth))

    def store_piece(terms):
        def store(at, value):
            for slot in terms:
                value += line_in[slot, at].astype(F32)
            piece_ref[at] = value.astype(BF16)

        pair_total(depth - 1, store)

    pl.when(z == 0)(lambda: store_piece([depth]))
    pl.when(z == depth - 1)(lambda: store_piece([z]))
    pl.when(inner > 0)(lambda: store_piece([z, depth]))
    for t in range(depth):
        for copy in pair_copies(t):
            copy.wait_send()
    for t in range(depth - 1):
        line_copy(t).wait_send()
    weights.finish()
    to_rows.finish()


def backward_exchange(
    slot_of, place_of, qkv, out_t, total, grad_mixed, grad_mixing, part_out,
    grad_shrink, grad_expand, normed, w_attend, heads, sizes,
):
    fsdp, n = sizes
    length = qkv.shape[0]
    rows, lanes = length // n, heads * HD
    width = grad_mixed.shape[1]
    own = width // fsdp
    hidden = grad_expand.shape[1]
    small = own // n
    if sizes != (4, 8):
        grad_heads = ctx_to_heads(grad_mixed, n).reshape(length, lanes)
        d_qkv = attend_backward(slot_of, place_of, qkv, grad_heads, out_t, total, heads)
        shrink = lax.psum_scatter(grad_shrink, "ctx", scatter_dimension=0, tiled=True)
        expand = lax.psum_scatter(
            grad_expand.reshape(fsdp, n, small, hidden)
            .transpose(1, 0, 2, 3)
            .reshape(n * fsdp * small, hidden),
            "ctx",
            scatter_dimension=0,
            tiled=True,
        )
        joint = (
            ctx_to_rows(d_qkv.reshape(n, rows, 3 * lanes))
            .reshape(rows, n, 3, lanes)
            .transpose(0, 2, 1, 3)
            .reshape(rows, 3 * width)
        )
        return (
            joint,
            lax.psum_scatter(grad_mixing, "fsdp", scatter_dimension=0, tiled=True),
            lax.psum_scatter(part_out, "fsdp", scatter_dimension=0, tiled=True).astype(F32),
            shrink,
            expand.reshape(fsdp, small, hidden),
            lax.psum_scatter(
                dot_first(normed, d_qkv).astype(BF16), "fsdp", scatter_dimension=0, tiled=True
            ),
            lax.all_gather(w_attend, "fsdp", axis=0, tiled=True),
        )
    half = hidden // n
    tall = half + fsdp * small
    depth = n // 2
    count = 4 * (n - 1) + 3 * (2 * CHUNKS + 1) + 5
    vmem, anywhere = pl.BlockSpec(memory_space=pltpu.VMEM), pl.BlockSpec(memory_space=pl.ANY)
    smem = pl.BlockSpec(memory_space=pltpu.SMEM)
    joint, own_mixing, branch, piece, own_attend, whole_attend = pl.pallas_call(
        functools.partial(backward_kernel, n, heads),
        out_shape=(
            jax.ShapeDtypeStruct((rows, 3 * width), BF16),
            jax.ShapeDtypeStruct((own, width), BF16),
            jax.ShapeDtypeStruct((rows, width), F32),
            jax.ShapeDtypeStruct((tall, width), BF16),
            jax.ShapeDtypeStruct((own, 3 * lanes), BF16),
            jax.ShapeDtypeStruct((fsdp,) + w_attend.shape, BF16),
        ),
        in_specs=[smem, smem] + [vmem] * 8 + [anywhere] * 2,
        out_specs=(anywhere, vmem, vmem, vmem, vmem, anywhere),
        scratch_shapes=attend_backward_scratch(length, heads)
        + [
            pltpu.VMEM((length, 3 * lanes), BF16),
            pltpu.VMEM((n, rows, lanes), BF16),
            pltpu.VMEM((length, width), BF16),
            pltpu.VMEM((fsdp, own, 3 * lanes), BF16),
        ]
        + scatter_buffers(own, width)
        + scatter_buffers(rows, width)
        + scatter_buffers(own, 3 * lanes)
        + [
            pltpu.VMEM((depth, tall, width), BF16),
            pltpu.VMEM((depth - 1, tall, width), BF16),
            pltpu.VMEM((depth + 1, tall, width), BF16),
            pltpu.SemaphoreType.DMA,
            pltpu.SemaphoreType.DMA((5,)),
            pltpu.SemaphoreType.DMA((count,)),
            pltpu.SemaphoreType.DMA((count,)),
            pltpu.SemaphoreType.DMA((depth, 1 + fsdp)),
            pltpu.SemaphoreType.DMA((depth, 1 + fsdp)),
            pltpu.SemaphoreType.DMA((depth - 1,)),
            pltpu.SemaphoreType.DMA((depth + 1,)),
        ],
        compiler_params=pltpu.CompilerParams(
            collective_id=6, has_side_effects=True, vmem_limit_bytes=VMEM_LIMIT
        ),
    )(
        slot_of,
        place_of,
        qkv,
        out_t,
        total,
        grad_mixed,
        grad_mixing.reshape(fsdp, own, width),
        part_out.reshape(fsdp, rows, width),
        grad_shrink.reshape(n, half, width),
        grad_expand.reshape(fsdp, n, small, hidden),
        normed,
        w_attend,
    )
    return (
        joint,
        own_mixing,
        branch,
        piece[:half],
        piece[half:].reshape(fsdp, small, width),
        own_attend,
        whole_attend.reshape(width, 3 * width),
    )


def dot_last(left, right):
    return lax.dot_general(left, right, (((1,), (1,)), ((), ())), preferred_element_type=F32)


def dot_first(left, right):
    return lax.dot_general(left, right, (((0,), (0,)), ((), ())), preferred_element_type=F32)


def middle_kernel(
    n, heads_ref, start_ref, norms_ref, mixing_ref, expand_ref, shrink_ref, grads_ref,
    middle_ref, grad_middle_ref, grad_mixed_ref, sums_ref,
    grad_mixing_ref, part_out_ref, grad_shrink_ref, grad_expand_ref,
    w_mixing, w_expand, w_shrink, grads, mixed, normal, inverse, own_two, normed,
    activated, grad_expanded, part_two, part_out, grad_mixing, grad_shrink, grad_expand,
    branch, near_buf, far_out, far_in,
    load_sems, store_sems, local_sems, send_sems, recv_sems,
):
    f, c, x, k, mate, across = fsdp_partners()
    rows, width = start_ref.shape
    lanes = heads_ref.shape[-1]
    hidden = w_expand.shape[1]
    everything = normed.shape[0] * rows
    loads = [
        pltpu.make_async_copy(src, dst, load_sems.at[j])
        for j, (src, dst) in enumerate(
            (
                (mixing_ref, w_mixing),
                (expand_ref, w_expand),
                (shrink_ref, w_shrink),
                (grads_ref, grads),
            )
        )
    ]
    stores = [
        pltpu.make_async_copy(src, dst, store_sems.at[j])
        for j, (src, dst) in enumerate(
            (
                (part_out, part_out_ref),
                (grad_shrink, grad_shrink_ref),
                (grad_expand, grad_expand_ref),
                (grad_mixing, grad_mixing_ref),
            )
        )
    ]
    for copy in loads:
        copy.start()
    greet_ctx(n, [(mate, c), (across, c)])
    pieces = Pieces(send_sems, recv_sems)
    to_rows = CtxExchange(
        pieces, n, lambda j: [heads_ref.at[j]], lambda j: [column_block(mixed, j, lanes)],
        [local_sems.at[0]],
    )
    gather = FsdpGather(pieces, own_two, normed, local_sems.at[1])
    scatter = FsdpScatter(pieces, part_two, near_buf, far_out, far_in)
    to_rows.start()
    loads[0].wait()
    to_rows.finish()

    gain, shift = norms_ref[2:3, :], norms_ref[3:4, :]
    middle_ref[...] = start_ref[...].astype(F32) + dot(mixed[...], w_mixing[...])

    @pl.loop(0, rows // 64)
    def _(t):
        part = pl.ds(pl.multiple_of(t * 64, 64), 64)
        one, scale = norm_parts(middle_ref[part])
        normal[part] = one
        inverse[part] = jnp.broadcast_to(scale, (64, 128))
        own_two[part] = (one * gain + shift).astype(BF16)

    gather.start()
    for copy in loads[1:]:
        copy.wait()

    @pl.loop(0, 4)
    def _(t):
        b = (x + t // 2) % 2 * 2 + (k + t) % 2

        @pl.when(t == 0)
        def _():
            gather.local.wait()

        @pl.when(t == 1)
        def _():
            gather.near.wait_recv()

        @pl.when(t == 2)
        def _():
            gather.forward()

        @pl.when(t == 3)
        def _():
            for copy in gather.passed:
                copy.wait_recv()

        @pl.loop(0, hidden // TILE)
        def _(j):
            cols = pl.ds(pl.multiple_of(j * TILE, TILE), TILE)
            value, slope = gelu_and_slope(dot(normed[b], w_expand[:, cols]))
            grad = dot_last(grads[b], w_shrink[cols, :]).astype(BF16).astype(F32)
            activated[b, :, cols] = value.astype(BF16)
            grad_expanded[b, :, cols] = (grad * slope).astype(BF16)

        @pl.loop(0, width // TILE)
        def _(j):
            cols = pl.ds(pl.multiple_of(j * TILE, TILE), TILE)
            part_two[b, :, cols] = dot_last(grad_expanded[b], w_expand[cols, :]).astype(BF16)

    scatter.start()
    scatter.forward()

    @pl.loop(0, 4)
    def _(b):
        @pl.loop(0, width // TILE)
        def _(j):
            cols = pl.ds(pl.multiple_of(j * TILE, TILE), TILE)
            part_out[b, :, cols] = dot(activated[b], w_shrink[:, cols]).astype(BF16)

    stores[0].start()

    @pl.loop(0, hidden // TILE)
    def _(j):
        cols = pl.ds(pl.multiple_of(j * TILE, TILE), TILE)
        grad_shrink[cols, :] = dot_first(
            activated[:, :, cols].reshape(everything, TILE), grads[...].reshape(everything, width)
        ).astype(BF16)

    stores[1].start()

    @pl.loop(0, width // TILE)
    def _(j):
        cols = pl.ds(pl.multiple_of(j * TILE, TILE), TILE)
        grad_expand[cols, :] = dot_first(
            normed[:, :, cols].reshape(everything, TILE),
            grad_expanded[...].reshape(everything, hidden),
        ).astype(BF16)

    stores[2].start()
    sums_ref[...] = jnp.zeros_like(sums_ref)

    def store(p, err):
        one = normal[p]
        sums_ref[2:3, :] += jnp.sum(err * one, axis=0, keepdims=True)
        sums_ref[3:4, :] += jnp.sum(err, axis=0, keepdims=True)
        total = grads[f, p].astype(F32) + norm_back(err, gain, one, inverse[p, :1])
        grad_middle_ref[p] = total
        branch[p] = total.astype(BF16)

    scatter.finish(store)
    grad_mixed_ref[...] = dot_last(branch[...], w_mixing[...]).astype(BF16)

    @pl.loop(0, width // TILE)
    def _(j):
        cols = pl.ds(pl.multiple_of(j * TILE, TILE), TILE)
        grad_mixing[cols, :] = dot_first(mixed[:, cols], branch[...]).astype(BF16)

    stores[3].start()
    gather.near.wait_send()
    for copy, onward in zip(gather.far, gather.passed):
        copy.wait_send()
        onward.wait_send()
    for copy in stores:
        copy.wait()


def middle_stage(mixed_heads, start, norms, whole_mixing, expand_columns, w_shrink, grads_in, sizes):
    fsdp, n = sizes
    rows, width = start.shape
    lanes = width // n
    hidden = w_shrink.shape[0]
    if sizes != (4, 8):
        mixed = ctx_to_rows(mixed_heads.reshape(n, rows, lanes))
        middle = start.astype(F32) + dot(mixed, whole_mixing)
        normal, inverse = norm_parts(middle)
        own_two = (normal * norms[2] + norms[3]).astype(BF16)
        normed = lax.all_gather(own_two, "fsdp", axis=0, tiled=True)
        activated, slope = gelu_and_slope(dot(normed, expand_columns))
        activated = activated.astype(BF16)
        grad = dot_last(grads_in, w_shrink).astype(BF16).astype(F32)
        grad_expanded = (grad * slope).astype(BF16)
        part_two = dot_last(grad_expanded, expand_columns).astype(BF16)
        err = lax.psum_scatter(part_two, "fsdp", scatter_dimension=0, tiled=True).astype(F32)
        f = lax.axis_index("fsdp")
        incoming = lax.dynamic_slice_in_dim(grads_in, f * rows, rows, 0)
        grad_middle = incoming.astype(F32) + norm_back(err, norms[2], normal, inverse)
        branch = grad_middle.astype(BF16)
        zero = jnp.zeros((width,), F32)
        sums = jnp.stack(
            [zero, zero, jnp.sum(err * normal, axis=0), jnp.sum(err, axis=0)] + [zero] * 4
        )
        return (
            middle,
            grad_middle,
            dot_last(branch, whole_mixing).astype(BF16),
            sums,
            dot_first(mixed, branch).astype(BF16),
            dot(activated, w_shrink).astype(BF16),
            dot_first(activated, grads_in).astype(BF16),
            dot_first(normed, grad_expanded).astype(BF16),
        )
    vmem, anywhere = pl.BlockSpec(memory_space=pltpu.VMEM), pl.BlockSpec(memory_space=pl.ANY)
    count = n - 1 + 2 * (2 * CHUNKS + 1)
    blocks = pltpu.VMEM((fsdp, rows, width), BF16)
    hidden_blocks = pltpu.VMEM((fsdp, rows, hidden), BF16)
    result = pl.pallas_call(
        functools.partial(middle_kernel, n),
        out_shape=(
            jax.ShapeDtypeStruct((rows, width), F32),
            jax.ShapeDtypeStruct((rows, width), F32),
            jax.ShapeDtypeStruct((rows, width), BF16),
            jax.ShapeDtypeStruct((8, width), F32),
            jax.ShapeDtypeStruct((width, width), BF16),
            jax.ShapeDtypeStruct((fsdp, rows, width), BF16),
            jax.ShapeDtypeStruct((hidden, width), BF16),
            jax.ShapeDtypeStruct((width, hidden), BF16),
        ),
        in_specs=[vmem] * 3 + [anywhere] * 4,
        out_specs=(vmem,) * 4 + (anywhere,) * 4,
        scratch_shapes=[
            pltpu.VMEM((width, width), BF16),
            pltpu.VMEM((width, hidden), BF16),
            pltpu.VMEM((hidden, width), BF16),
            blocks,
            pltpu.VMEM((rows, width), BF16),
            pltpu.VMEM((rows, width), F32),
            pltpu.VMEM((rows, 128), F32),
            pltpu.VMEM((rows, width), BF16),
            blocks,
            hidden_blocks,
            hidden_blocks,
            blocks,
            blocks,
            pltpu.VMEM((width, width), BF16),
            pltpu.VMEM((hidden, width), BF16),
            pltpu.VMEM((width, hidden), BF16),
            pltpu.VMEM((rows, width), BF16),
        ]
        + scatter_buffers(rows, width)
        + [
            pltpu.SemaphoreType.DMA((4,)),
            pltpu.SemaphoreType.DMA((4,)),
            pltpu.SemaphoreType.DMA((2,)),
            pltpu.SemaphoreType.DMA((count,)),
            pltpu.SemaphoreType.DMA((count,)),
        ],
        compiler_params=pltpu.CompilerParams(
            collective_id=4, has_side_effects=True, vmem_limit_bytes=VMEM_LIMIT
        ),
    )(
        mixed_heads.reshape(n, rows, lanes),
        start,
        norms,
        whole_mixing,
        expand_columns,
        w_shrink,
        grads_in.reshape(fsdp, rows, width),
    )
    middle, grad_middle, grad_mixed, sums, grad_mixing, part_out, grad_shrink, grad_expand = result
    return (
        middle,
        grad_middle,
        grad_mixed,
        sums,
        grad_mixing,
        part_out.reshape(fsdp * rows, width),
        grad_shrink,
        grad_expand,
    )


def shards(
    sizes,
    tokens,
    out_grad,
    slot_block,
    w_attend,
    w_mixing,
    w_expand,
    w_shrink,
    w_norms,
    first_attend,
    first_mixing,
    first_expand,
    first_shrink,
    first_norms,
    second_attend,
    second_mixing,
    second_expand,
    second_shrink,
    second_norms,
):
    fsdp, ctx = sizes
    f, c = lax.axis_index("fsdp"), lax.axis_index("ctx")
    rows, width = tokens.shape[1:]
    heads = width // HD // ctx
    lanes = heads * HD
    length = rows * ctx
    own = width // fsdp
    hidden = w_shrink.shape[0]

    place_of = slot_block[0]
    slot_of = jnp.sum(
        jnp.where(
            place_of[None, :] == jnp.arange(2 * ctx, dtype=jnp.int32)[:, None],
            jnp.arange(2 * ctx, dtype=jnp.int32)[None, :],
            0,
        ),
        axis=1,
    )

    start = tokens[0]
    incoming = out_grad[0]
    padded_norms = jnp.concatenate([w_norms.astype(F32), jnp.zeros((4, own), F32)], axis=0)
    mixed_heads, out_t, total, qkv, norms, normed_all, expand_columns, whole_mixing, grads_in = (
        forward_stage(
            slot_of, place_of, start, w_attend, padded_norms, w_expand, w_mixing, incoming,
            hidden, heads, sizes,
        )
    )
    (
        middle,
        grad_middle,
        grad_mixed,
        norm_sums,
        grad_mixing,
        part_out,
        grad_shrink,
        grad_expand,
    ) = middle_stage(
        mixed_heads, start, norms, whole_mixing, expand_columns, w_shrink, grads_in, sizes
    )
    joint, own_mixing, branch, shrink_piece, expand_piece, own_attend, whole_attend = (
        backward_exchange(
            slot_of, place_of, qkv, out_t, total, grad_mixed, grad_mixing, part_out,
            grad_shrink, grad_expand, normed_all, w_attend, heads, sizes,
        )
    )
    layer_out = (middle + branch).astype(BF16)
    sum_attend, sum_mixing, parts_norms, sum_shrink, sum_expand, back = last_exchange(
        own_attend, own_mixing, norm_sums, shrink_piece, expand_piece, joint, whole_attend,
        start, norms, sizes,
    )
    tokens_grad = (grad_middle + back)[None]
    sum_attend, sum_mixing = sum_attend.astype(F32), sum_mixing.astype(F32)
    sum_shrink, sum_expand = sum_shrink.astype(F32), sum_expand.astype(F32)
    sum_norms = jnp.sum(parts_norms, axis=0)[:4]

    result = [layer_out[None], tokens_grad]
    for weight, grad, first, second in (
        (w_attend, sum_attend, first_attend, second_attend),
        (w_mixing, sum_mixing, first_mixing, second_mixing),
        (w_expand, sum_expand, first_expand, second_expand),
        (w_shrink, sum_shrink, first_shrink, second_shrink),
        (w_norms, sum_norms, first_norms, second_norms),
    ):
        result.append(grad)
        result.extend(adam_step(weight, grad, first, second))
    return tuple(result)


def solution(mesh):
    rows = P("fsdp", None)
    columns = P(None, "fsdp")
    tokens = P("fsdp", "ctx", None)
    return jax.shard_map(
        functools.partial(shards, (mesh.shape["fsdp"], mesh.shape["ctx"])),
        mesh=mesh,
        in_specs=(tokens, tokens, rows)
        + (rows, rows, rows, rows, columns) * 3,
        out_specs=(tokens, tokens) + (rows,) * 16 + (columns,) * 4,
        check_vma=False,
    )
```
